32 devices in a mesh: expert: 8 (over y, x, core), mp: 4 (over z).
Axes of the slice: x: 2, y: 2, z: 4, core: 2. Of those that a mesh axis runs over, the one named last changes fastest.
Arguments:
- tokens: bfloat16 [1024, 7168], P('expert', 'mp'), may hold values from -0.625 to 0.625
- cotangent: bfloat16 [1024, 8, 2048], P('expert', None, 'mp'), may hold values from -3 to 3
- weights: bfloat16 [16, 7168, 2048], P('expert', 'mp'), may hold values from -0.0625 to 0.0625
- steps: float32 [16, 2048], P('expert', 'mp'), may hold values from 0.002 to 0.02
- expert_ids: int32 [1024, 8], P('expert'), may hold values from 0 to 15, all different within a row; in each aligned block of 128 rows (0 to 127, 128 to 255, ...) at most 64 rows name the same one
Outputs:
- token_grads: bfloat16 [1024, 7168], P('expert', 'mp')
- weight_grads: bfloat16 [16, 7168, 2048], P('expert', 'mp')
- step_grads: float32 [16, 2048], P('expert', 'mp')
The draws below stay inside these ranges and needn't reach their ends.
Inputs may be any that keep to these rules, and one draw needn't show every extreme that they name: `expert_ids`: each row names 8 different experts; among the 128 rows of one index of the expert axis, no expert is named by more than 64 rows, a bound that some block reaches of them.
All inputs are finite; a program needn't handle non-finite values.
Results may differ from the reference program's by a relative error of at most 0.0058.
Values may be sent and summed in bfloat16 or wider, within the bound.
No kernel may reach another device: no remote copies, remote signals or barrier semaphores. Data moves between devices by JAX's collectives and lax.ppermute only.
A program may use at most 128 MiB of HBM per device.

```python
import math
import jax
import jax.numpy as jnp
import numpy as np
from jax import lax

D = 7168
FF = 2048
TOP = 8
TOK_DEV = 128
EXPERTS = 16
CAP = 64
TOKENS = 1024
N_EXPERT = 8


def level_of(stream_key, shape, shards, smallest, largest):
    level, own = 1.0, jax.random.fold_in(stream_key, 6)
    for dim, shards_of in shards:
        draws = jnp.exp(jax.random.uniform(jax.random.fold_in(own, dim), (shards_of,), jnp.float32, smallest / len(shards), largest / len(shards)))
        level = level * jnp.repeat(draws, shape[dim] // shards_of).reshape([-1 if axis == dim else 1 for axis in range(len(shape))])
    return level


def assign_block(rng, own, number, rows, number_of, top, bound, skew):
    sequence = jax.random.permutation(rng, number_of)
    heavy_load, common = shares(number_of, rows * top, bound, skew, True), shares(number_of, rows * top, bound, skew, False)
    places = jnp.arange(number_of)

    def named(sizes, rotation):
        used = int((sizes > 0).sum())
        fixed = max(1, used // 4)
        moved = fixed + (places - fixed + rotation * (used - fixed)) % max(1, number_of - fixed)
        return jnp.zeros((number_of,), jnp.int32).at[sequence[jnp.where(places < fixed, places, moved)]].set(jnp.asarray(sizes, jnp.int32))

    sizes = jnp.where(number % 4 == 0, named(heavy_load, number // 4), named(common, number - number // 4 - 1))
    mixed = jax.random.permutation(jax.random.fold_in(own, 3), number_of)
    donor, taker = mixed[0:number_of // 2 * 2:2], mixed[1:number_of // 2 * 2:2]
    room = jnp.minimum(sizes[donor] - 1, bound - sizes[taker]) // 2
    room = jnp.where((donor == sequence[0]) | (taker == sequence[0]) | (sizes[taker] == 0), 0, jnp.maximum(room, 0))
    moved = jax.random.randint(jax.random.fold_in(own, 4), (number_of // 2,), 0, 1 << 20) % (room + 1)
    sizes = sizes.at[donor].add(-moved).at[taker].add(moved)
    items = jnp.searchsorted(jnp.cumsum(sizes), jnp.arange(rows * top), side="right").astype(jnp.int32)
    table = items.reshape(top, rows).T
    table = table[jax.random.permutation(jax.random.fold_in(own, 1), rows)]
    rotation = jax.random.randint(jax.random.fold_in(own, 2), (rows, 1), 0, top)
    return jnp.take_along_axis(table, (jnp.arange(top)[None, :] + rotation) % top, axis=1)


def shares(number_of, total, bound, slope, full):
    weights = [(1 << 20) // math.isqrt(grade ** slope) + 1 for grade in range(1, number_of + 1)]
    largest = bound if full else min(bound, max(-(-total // number_of), total * weights[0] // sum(weights)))
    least = 1 if total - largest >= number_of - 1 else 0
    given, rest = [largest] + [least] * (number_of - 1), total - largest - least * (number_of - 1)
    while rest > 0:
        movable = [i for i in range(1, number_of) if given[i] < largest] or [i for i in range(1, number_of) if given[i] < bound]
        whole, left = sum([weights[i] for i in movable]), rest
        for i in movable:
            more = min(bound - given[i], max(1, left * weights[i] // whole), rest)
            given[i] = given[i] + more
            rest = rest - more
    return np.array(given)


def normal_values(own_key, extent, scale, reach, shards=(), kind=jnp.bfloat16):
    result = scale * jax.random.normal(own_key, extent, jnp.float32)
    if shards:
        result = result * level_of(own_key, extent, shards, -0.22, 0.18)
    return jnp.clip(result, -reach, reach).astype(kind)


def setup_inputs(seed: int = 0) -> dict:
    splits = jax.random.split(jax.random.key(seed), 6)
    tokens = normal_values(splits[0], (TOKENS, D), 0.1, 0.625, ((0, 8), (1, 4)))
    cotangent = normal_values(splits[1], (TOKENS, TOP, FF), 0.5, 3.0, ((0, 8), (2, 4)))
    weights = normal_values(splits[2], (EXPERTS, D, FF), D ** -0.5, 0.0625, ((0, 8), (1, 4)))
    steps = jnp.clip(jnp.exp(math.log(0.02) - 2.30258502 * jax.random.uniform(splits[3], (EXPERTS, FF), jnp.float32) ** level_of(splits[3], (EXPERTS, FF), ((0, 8), (1, 4)), -0.2, 0.2)), 0.002, 0.02)
    expert_ids_keys = jax.random.split(jax.random.fold_in(splits[4], 1), TOKENS // TOK_DEV)
    expert_ids_turns = jax.random.permutation(jax.random.fold_in(splits[4], 3), TOKENS // TOK_DEV)
    expert_ids = jax.vmap(lambda own, number: assign_block(jax.random.fold_in(splits[4], 2), own, number, TOK_DEV, EXPERTS, TOP, CAP, 2))(expert_ids_keys, expert_ids_turns).reshape((TOKENS, TOP))
    return dict(tokens=tokens, cotangent=cotangent, weights=weights, steps=steps, expert_ids=expert_ids)


qmax = 7.0
wiggle = 0.9
two_pi = 6.283185307179586

def quantize(weight_f, step_f):
    scaled = weight_f / step_f
    squash = jnp.tanh(scaled / qmax)
    clipped = qmax * squash
    angles = two_pi * clipped
    stair = clipped - wiggle * jnp.sin(angles) / two_pi
    slopes = (1.0 - wiggle * jnp.cos(angles)) * (1.0 - squash * squash)
    return (step_f * stair, slopes, stair - scaled * slopes)

def slot_table(routes_flat, experts, capacity):
    one_hot = (routes_flat[:, None] == jnp.arange(experts, dtype=jnp.int32)[None, :]).astype(jnp.int32)
    before = jnp.cumsum(one_hot, axis=0) - one_hot
    position = lax.optimization_barrier(jnp.sum(before * one_hot, axis=1))
    slot_of = (routes_flat * capacity + position).astype(jnp.int32)
    route_count = routes_flat.shape[0]
    source_of = jnp.full((experts * capacity,), route_count, jnp.int32)
    source_of = source_of.at[slot_of].set(jnp.arange(route_count, dtype=jnp.int32))
    return (slot_of, source_of)

def reference(tokens, cotangent, weights, steps, expert_ids):
    blocks = expert_ids.reshape(N_EXPERT, TOK_DEV * TOP)
    sources = jax.vmap(lambda block_rows: slot_table(block_rows, EXPERTS, CAP)[1])(blocks)
    offsets = (jnp.arange(N_EXPERT, dtype=jnp.int32) * (TOK_DEV * TOP))[:, None]
    sentinel = TOKENS * TOP
    global_src = jnp.where(sources < TOK_DEV * TOP, sources + offsets, sentinel).astype(jnp.int32)
    per_expert = global_src.reshape(N_EXPERT, EXPERTS, CAP).transpose(1, 0, 2).reshape(EXPERTS, N_EXPERT * CAP)
    padded_x = jnp.concatenate([tokens, jnp.zeros((1, D), tokens.dtype)], axis=0)
    padded_g = jnp.concatenate([cotangent.reshape(TOKENS * TOP, FF), jnp.zeros((1, FF), cotangent.dtype)], axis=0)
    grad_scale = 1.0 / math.sqrt(D * qmax)

    def one_expert(running, inputs):
        weight_e, step_e, route_e = inputs
        token_e = (route_e // TOP).astype(jnp.int32)
        rows_x = padded_x[token_e]
        rows_g = padded_g[route_e]
        levels, slopes, step_slopes = quantize(weight_e.astype(jnp.float32), step_e[None, :])
        quantized = levels.astype(jnp.bfloat16)
        raw = jnp.dot(rows_x.T, rows_g, preferred_element_type=jnp.float32)
        out_weight = (raw * slopes).astype(jnp.bfloat16)
        out_step = grad_scale * lax.optimization_barrier(jnp.sum(raw * step_slopes, axis=0))
        back = jnp.dot(rows_g, quantized.T, preferred_element_type=jnp.float32).astype(jnp.bfloat16)
        running = running.at[token_e].add(back.astype(jnp.float32))
        return (running, (out_weight, out_step))
    start_sum = jnp.zeros((TOKENS + 1, D), jnp.float32)
    summed, (weight_grads, step_grads) = lax.scan(one_expert, start_sum, (weights, steps, per_expert))
    return (summed[:TOKENS].astype(jnp.bfloat16), weight_grads, step_grads)
```

```python
import math

import jax
import jax.numpy as jnp
from jax import lax
from jax.experimental import pallas as pl
from jax.experimental.pallas import tpu as pltpu
from jax.sharding import PartitionSpec as P

QMAX = 7.0
WIGGLE = 0.9
BF16 = jnp.bfloat16
F32 = jnp.float32

SIN = (
    3.141592580044724,
    -5.167706878926178,
    2.5500313772770724,
    -0.5980451741027515,
    0.07722012891724155,
)
ROUNDER = 12582912.0


def params(mib=48):
    return pltpu.CompilerParams(vmem_limit_bytes=mib * 1024 * 1024)


def partner(offset, index, size):
    if size & (size - 1) == 0:
        return index ^ offset
    return (offset - index) % size


def swap(x, axis, offset, size):
    return lax.ppermute(x, axis, [(i, partner(offset, i, size)) for i in range(size)])


def row_tile(rows, want):
    tile = min(rows, want)
    while rows % tile:
        tile //= 2
    return tile


def quantize_piece(which, weights, steps, j, part):
    _, width, _ = weights.shape
    dt = row_tile(width, 448)
    chunk = row_tile(dt, 16)

    def kernel(which_ref, w_ref, s_ref, q_ref, sl_ref, ts_ref):
        step = s_ref[j : j + 1, :]
        inv = 1.0 / (QMAX * step)
        step7 = QMAX * step

        def body(i, carry):
            rows = pl.ds(pl.multiple_of(i * chunk, chunk), chunk)
            t = w_ref[0, rows, :].astype(F32) * inv
            u = jnp.tanh(t)
            c = QMAX * u
            r = c - ((c + ROUNDER) - ROUNDER)
            y = r * r
            poly = SIN[4]
            for k in SIN[3::-1]:
                poly = poly * y + k
            sine = r * poly
            z = sine * sine
            x = 1.0000005 - z
            cosine = x * lax.rsqrt(x)
            level = u - (WIGGLE / (math.pi * QMAX)) * (sine * cosine)
            slopes = (1.0 - WIGGLE + 2.0 * WIGGLE * z) * (1.0 - u * u)
            q_ref[rows, :] = (step7 * level).astype(BF16)
            sl_ref[rows, :] = slopes.astype(BF16)
            ts_ref[rows, :] = (level - t * slopes).astype(BF16)
            return carry

        lax.fori_loop(0, dt // chunk, body, 0)

    return pl.pallas_call(
        kernel,
        grid_spec=pltpu.PrefetchScalarGridSpec(
            num_scalar_prefetch=1,
            grid=(width // dt,),
            in_specs=[
                pl.BlockSpec((1, dt, part), lambda i, which: (j, i, which[0])),
                pl.BlockSpec(steps.shape, lambda i, which: (0, 0)),
            ],
            out_specs=[pl.BlockSpec((dt, part), lambda i, which: (i, 0))] * 3,
        ),
        out_shape=[jax.ShapeDtypeStruct((width, part), BF16)] * 3,
        compiler_params=params(),
        name="quantize",
    )(which, weights, steps)


def earlier(n):
    rows = lax.broadcasted_iota(jnp.int32, (n, n), 0)
    return (rows < lax.broadcasted_iota(jnp.int32, (n, n), 1)).astype(F32).astype(BF16)


def dispatch(me, ids_row, cot, groups, local, capacity):
    routes, part = cot.shape
    experts = groups * local

    def kernel(me_ref, ids_ref, cot_ref, *refs):
        outs, code_ref = refs[:-1], refs[-1]
        ids = ids_ref[...]
        expert = lax.broadcasted_iota(jnp.int32, (experts, routes), 0)
        named = expert == ids
        before = jnp.dot(named.astype(F32).astype(BF16), earlier(routes), preferred_element_type=F32)
        code_ref[...] = jnp.where(named, before.astype(jnp.int32), -1)
        slot = lax.broadcasted_iota(jnp.int32, (capacity, routes), 0)
        for n in range(local * groups):
            j, k = n // groups, n % groups
            e = partner(k, me_ref[0], groups) * local + j
            pick = (slot == code_ref[pl.ds(e, 1), :]).astype(F32).astype(BF16)
            outs[n][...] = jnp.dot(pick, cot_ref[...], preferred_element_type=F32).astype(BF16)

    outs = pl.pallas_call(
        kernel,
        grid_spec=pltpu.PrefetchScalarGridSpec(
            num_scalar_prefetch=1,
            grid=(1,),
            in_specs=[
                pl.BlockSpec(ids_row.shape, lambda i, me: (0, 0)),
                pl.BlockSpec(cot.shape, lambda i, me: (0, 0)),
            ],
            out_specs=[pl.BlockSpec((capacity, part), lambda i, me: (0, 0))] * (local * groups),
            scratch_shapes=[pltpu.VMEM((experts, routes), jnp.int32)],
        ),
        out_shape=[jax.ShapeDtypeStruct((capacity, part), BF16)] * (local * groups),
        compiler_params=params(),
        name="dispatch",
    )(me, ids_row, cot)
    return [outs[j * groups : (j + 1) * groups] for j in range(local)]


def expert_rows(me, blocks, groups, local, tok_rows, capacity, top_k):
    width = blocks[0].shape[1]
    dt = row_tile(width, 256)

    def kernel(me_ref, *refs):
        ins, outs, pick_ref = refs[:groups], refs[groups:-1], refs[-1]

        ids_refs, ins = ins, refs[groups : 2 * groups]
        outs = refs[2 * groups : -1]

        @pl.when(pl.program_id(0) == 0)
        def _():
            upper = earlier(tok_rows)
            slot = lax.broadcasted_iota(jnp.int32, (capacity, tok_rows), 0)
            for j in range(local):
                e = (me_ref[0] * local + j).astype(F32)
                for k in range(groups):
                    ids = ids_refs[k][tok_rows : tok_rows + top_k, :tok_rows].astype(F32)
                    named = jnp.sum((ids == e).astype(F32), axis=0, keepdims=True)
                    before = jnp.dot(
                        jnp.broadcast_to(named, (8, tok_rows)).astype(BF16),
                        upper,
                        preferred_element_type=F32,
                    )[:1]
                    code = jnp.where(named > 0.5, before, -1.0).astype(jnp.int32)
                    pick_ref[j, k] = (slot == code).astype(F32).astype(BF16)

        for j in range(local):
            rows = jnp.concatenate(
                [
                    jnp.dot(pick_ref[j, k], ins[k][:tok_rows, :], preferred_element_type=F32)
                    for k in range(groups)
                ],
                axis=0,
            )
            outs[j][...] = rows.T.astype(BF16)

    rows_in = blocks[0].shape[0]
    return pl.pallas_call(
        kernel,
        grid_spec=pltpu.PrefetchScalarGridSpec(
            num_scalar_prefetch=1,
            grid=(width // dt,),
            in_specs=[pl.BlockSpec((rows_in, dt), lambda i, me: (0, 0))] * groups
            + [pl.BlockSpec((rows_in, dt), lambda i, me: (0, i))] * groups,
            out_specs=[pl.BlockSpec((dt, groups * capacity), lambda i, me: (i, 0))] * local,
            scratch_shapes=[pltpu.VMEM((local, groups, capacity, tok_rows), BF16)],
        ),
        out_shape=[jax.ShapeDtypeStruct((width, groups * capacity), BF16)] * local,
        compiler_params=params(),
        name="expert_rows",
    )(me, *blocks, *blocks)


def back_rows(grads, quantized, capacity):
    parts = len(grads)
    rows, part = grads[0].shape
    width = quantized[0].shape[0]
    dt = row_tile(width, 256)
    count = rows // capacity

    def kernel(*refs):
        total = None
        for g, q in zip(refs[:parts], refs[parts : 2 * parts]):
            term = lax.dot_general(
                g[...], q[...], (((1,), (1,)), ((), ())), preferred_element_type=F32
            )
            total = term if total is None else total + term
        for n, out in enumerate(refs[2 * parts :]):
            out[...] = total[n * capacity : (n + 1) * capacity].astype(BF16)

    return pl.pallas_call(
        kernel,
        grid=(width // dt,),
        in_specs=[pl.BlockSpec((rows, part), lambda i: (0, 0))] * parts
        + [pl.BlockSpec((dt, part), lambda i: (i, 0))] * parts,
        out_specs=[pl.BlockSpec((capacity, dt), lambda i: (0, i))] * count,
        out_shape=[jax.ShapeDtypeStruct((capacity, width), BF16)] * count,
        compiler_params=params(),
        name="back_rows",
    )(*grads, *quantized)


def weight_part(mine, rows_t, chunks, slopes, step_slopes, j, shape, scale, before):
    parts = len(slopes)
    width, part = slopes[0].shape
    dt = row_tile(width, 256)
    n_chunks = len(chunks)
    flat = [g for chunk in chunks for g in chunk]
    steps_in = 0 if before is None else 1

    def kernel(mine_ref, x_ref, *refs):
        gs = refs[: n_chunks * parts]
        sl = refs[n_chunks * parts :][:parts]
        ts = refs[n_chunks * parts + parts :][:parts]
        out, st = refs[n_chunks * parts + 2 * parts + steps_in :]
        i = pl.program_id(0)
        for r in range(parts):
            raw, at = None, 0
            for n in range(n_chunks):
                g = gs[n * parts + r]
                size = g.shape[0]
                term = jnp.dot(x_ref[:, at : at + size], g[...], preferred_element_type=F32)
                raw = term if raw is None else raw + term
                at += size
            column = pl.multiple_of(partner(r, mine_ref[0], parts) * part, part)
            out[0, :, pl.ds(column, part)] = (raw * sl[r][...].astype(F32)).astype(BF16)
            sums = jnp.sum((raw * ts[r][...].astype(F32)).reshape(dt // 8, 8, part), axis=0) * scale
            st[r] = jnp.where(i == 0, sums, st[r] + sums)

    return pl.pallas_call(
        kernel,
        grid_spec=pltpu.PrefetchScalarGridSpec(
            num_scalar_prefetch=1,
            grid=(width // dt,),
            in_specs=[pl.BlockSpec((dt, rows_t.shape[1]), lambda i, m: (i, 0))]
            + [pl.BlockSpec(g.shape, lambda i, m: (0, 0)) for g in flat]
            + [pl.BlockSpec((dt, part), lambda i, m: (i, 0))] * (2 * parts)
            + [pl.BlockSpec(memory_space=pl.ANY)] * steps_in,
            out_specs=[
                pl.BlockSpec((1, dt, parts * part), lambda i, m: (j, i, 0)),
                pl.BlockSpec((parts, 8, part), lambda i, m: (0, 0, 0)),
            ],
        ),
        out_shape=[
            jax.ShapeDtypeStruct(shape, BF16),
            jax.ShapeDtypeStruct((parts, 8, part), F32),
        ],
        input_output_aliases={2 + len(flat) + 2 * parts: 0} if steps_in else {},
        compiler_params=params(),
        name="weight_part",
    )(mine, rows_t, *flat, *slopes, *step_slopes, *(() if before is None else (before,)))


def combine(me, ids_t, returned, groups, local, capacity):
    top_k, tok_rows = ids_t.shape
    flat = [piece for of_expert in returned for piece in of_expert]
    width = flat[0].shape[1]
    dt = row_tile(width, 256)

    def kernel(me_ref, ids_ref, *refs):
        ins, out, pick_ref = refs[:-2], refs[-2], refs[-1]

        @pl.when(pl.program_id(0) == 0)
        def _():
            upper = earlier(tok_rows)
            slot = lax.broadcasted_iota(jnp.int32, (capacity, tok_rows), 0)
            ids = ids_ref[...]
            for n in range(local * groups):
                j, k = n // groups, n % groups
                e = partner(k, me_ref[0], groups) * local + j
                named = jnp.sum((ids == e.astype(F32)).astype(F32), axis=0, keepdims=True)
                before = jnp.dot(
                    jnp.broadcast_to(named, (8, tok_rows)).astype(BF16),
                    upper,
                    preferred_element_type=F32,
                )[:1]
                code = jnp.where(named > 0.5, before, -1.0).astype(jnp.int32)
                pick_ref[n * capacity : (n + 1) * capacity, :] = (slot == code).astype(F32).astype(BF16)

        rows = jnp.concatenate([r[...] for r in ins], axis=0)
        out[...] = lax.dot_general(
            pick_ref[...], rows, (((0,), (0,)), ((), ())), preferred_element_type=F32
        ).astype(BF16)

    return pl.pallas_call(
        kernel,
        grid_spec=pltpu.PrefetchScalarGridSpec(
            num_scalar_prefetch=1,
            grid=(width // dt,),
            in_specs=[pl.BlockSpec(ids_t.shape, lambda i, me: (0, 0))]
            + [pl.BlockSpec((capacity, dt), lambda i, me: (0, i))] * len(flat),
            out_specs=pl.BlockSpec((tok_rows, dt), lambda i, me: (0, i)),
            scratch_shapes=[pltpu.VMEM((len(flat) * capacity, tok_rows), BF16)],
        ),
        out_shape=jax.ShapeDtypeStruct((tok_rows, width), BF16),
        compiler_params=params(),
        name="combine",
    )(me, ids_t, *flat)


def per_device(tokens, cotangent, weights, steps, expert_ids):
    groups, parts = lax.axis_size("expert"), lax.axis_size("mp")
    local = weights.shape[0]
    tok_rows, top_k = expert_ids.shape
    capacity = tok_rows // 2
    part = cotangent.shape[2]
    width = tokens.shape[1]
    me, mine = lax.axis_index("expert"), lax.axis_index("mp")
    me_arr = me.astype(jnp.int32)[None]
    mine_arr = mine.astype(jnp.int32)[None]
    expert_swap = lambda x, k: swap(x, "expert", k, groups)
    mp_swap = lambda x, r: swap(x, "mp", r, parts)

    steps_of = [steps] + [mp_swap(steps, r) for r in range(1, parts)]
    ids_t = expert_ids.T.astype(F32)
    g_out = dispatch(
        me_arr,
        expert_ids.reshape(1, tok_rows * top_k),
        cotangent.reshape(tok_rows * top_k, part),
        groups,
        local,
        capacity,
    )
    g_in = [
        [g_out[j][0]] + [expert_swap(g_out[j][k], k) for k in range(1, groups)]
        for j in range(local)
    ]
    own = jnp.concatenate(
        [tokens, jnp.pad(ids_t.astype(BF16), ((0, 0), (0, width - tok_rows)))], axis=0
    )
    blocks = [own] + [None] * (groups - 1)
    for k in range(2, groups, 2):
        blocks[k] = expert_swap(own, k)
    for k in range(1, groups, 2):
        blocks[k] = expert_swap(blocks[k - 1], 1)
    half = groups // 2
    splits = [[list(range(groups))]] * (local - 1) + [[list(range(half, groups)), list(range(half))]]

    quantized = []
    for j in range(local):
        quantized.append(
            [
                quantize_piece(partner(r, mine, parts).astype(jnp.int32)[None], weights, steps_of[r], j, part)
                for r in range(parts)
            ]
        )
    rows_t = expert_rows(me_arr, blocks, groups, local, tok_rows, capacity, top_k)

    returned = [[None] * groups for _ in range(local)]
    weight_out, partial = None, []
    scale = QMAX / math.sqrt(width * parts * QMAX)
    for j in range(local):
        chunks, order = [], []
        for split in splits[j]:
            g0 = jnp.concatenate([g_in[j][k] for k in split], axis=0)
            chunk = [g0] + [mp_swap(g0, r) for r in range(1, parts)]
            chunks.append(chunk)
            backs = back_rows(chunk, [q[0] for q in quantized[j]], capacity)
            for k, piece in zip(split, backs):
                returned[j][k] = piece if k == 0 else expert_swap(piece, k)
        if len(splits[j]) > 1:
            chunks = chunks[::-1]
        weight_out, sums = weight_part(
            mine_arr,
            rows_t[j],
            chunks,
            [q[1] for q in quantized[j]],
            [q[2] for q in quantized[j]],
            j,
            weights.shape,
            scale,
            weight_out,
        )
        partial.append(sums)
    sums = jnp.stack([p.sum(axis=1) for p in partial], axis=1)
    step_out = sums[0]
    for r in range(1, parts):
        step_out = step_out + mp_swap(sums[r], r)
    token_out = combine(me_arr, ids_t, returned, groups, local, capacity)
    return (token_out, weight_out, step_out)


def solution(mesh):
    return jax.shard_map(
        per_device,
        mesh=mesh,
        in_specs=(
            P("expert", "mp"),
            P("expert", None, "mp"),
            P("expert", "mp", None),
            P("expert", "mp"),
            P("expert", None),
        ),
        out_specs=(P("expert", "mp"), P("expert", "mp", None), P("expert", "mp")),
        check_vma=False,
    )
```

```python
import math

import jax
import jax.numpy as jnp
from jax import lax
from jax.experimental import pallas as pl
from jax.experimental.pallas import tpu as pltpu
from jax.sharding import PartitionSpec as P


QMAX = 7.0
WIGGLE = 0.9
BF16 = jnp.bfloat16
F32 = jnp.float32

SIN = (
    3.141592580044724,
    -5.167706878926178,
    2.5500313772770724,
    -0.5980451741027515,
    0.07722012891724155,
)
SCALED = tuple(math.sqrt(2.0 * WIGGLE) * k for k in SIN)
ROUNDER = 12582912.0


def params(mib=48):
    return pltpu.CompilerParams(vmem_limit_bytes=mib * 1024 * 1024)


def partner(offset, index, size):
    if size & (size - 1) == 0:
        return index ^ offset
    return (offset - index) % size


def swap(x, axis, offset, size):
    return lax.ppermute(x, axis, [(i, partner(offset, i, size)) for i in range(size)])


def row_tile(rows, want):
    tile = min(rows, want)
    while rows % tile:
        tile //= 2
    return tile


def quantize(mine, weights, steps, at, j, low, high):
    parts = len(steps)
    rows_in = -(-3 * weights.shape[0] // 8) * 8
    _, width, full = weights.shape
    part = full // parts
    dt = row_tile(width, 896)
    chunk = row_tile(dt, 16)

    def kernel(mine_ref, w_ref, *refs):
        q_ref, sl_ref, ts_ref = refs[high - low :]
        thirds = refs[0][...].astype(F32)
        for r in range(1, high - low):
            thirds = jnp.where(pl.program_id(0) == r, refs[r][...].astype(F32), thirds)
        step = thirds[3 * j : 3 * j + 1] + thirds[3 * j + 1 : 3 * j + 2] + thirds[3 * j + 2 : 3 * j + 3]
        inv = 1.0 / (QMAX * step)
        step7 = QMAX * step

        def body(i, carry):
            rows = pl.ds(pl.multiple_of(i * chunk, chunk), chunk)
            t = w_ref[0, rows, :].astype(F32) * inv
            u = jnp.tanh(t)
            c = QMAX * u
            r = c - ((c + ROUNDER) - ROUNDER)
            y = r * r
            poly = SCALED[-1]
            for k in SCALED[-2::-1]:
                poly = poly * y + k
            sine = r * poly
            z = sine * sine
            x = 2.0 * WIGGLE * 1.0000005 - z
            cosine = x * lax.rsqrt(x)
            level = u - (0.5 / (math.pi * QMAX)) * (sine * cosine)
            slopes = (1.0 - WIGGLE + z) * (1.0 - u * u)
            q_ref[0, rows, :] = (step7 * level).astype(BF16)
            sl_ref[0, rows, :] = slopes.astype(BF16)
            ts_ref[0, rows, :] = (level - t * slopes).astype(BF16)
            return carry

        lax.fori_loop(0, dt // chunk, body, 0, unroll=2 if dt // chunk % 2 == 0 else 1)

    return pl.pallas_call(
        kernel,
        grid_spec=pltpu.PrefetchScalarGridSpec(
            num_scalar_prefetch=1,
            grid=(high - low, width // dt),
            in_specs=[
                pl.BlockSpec((1, dt, part), lambda r, i, mine: (j, i, partner(r + low, mine[0], parts))),
            ]
            + [pl.BlockSpec((rows_in, part), lambda r, i, mine: (at // rows_in, 0))] * (high - low),
            out_specs=[pl.BlockSpec((1, dt, part), lambda r, i, mine: (r, i, 0))] * 3,
        ),
        out_shape=[pltpu.HBM((high - low, width, part), BF16)] * 3,
        compiler_params=params(),
        name="quantize",
    )(mine, weights, *steps[low:high])


def picks(member, capacity):
    n, tok_rows = member.shape
    before = jnp.dot(member.astype(BF16), earlier(tok_rows), preferred_element_type=F32)
    code = jnp.where(member > 0.5, before, -1.0).astype(jnp.int32)
    slot = lax.broadcasted_iota(jnp.int32, (capacity, tok_rows), 0)
    rows = [(slot == code[i : i + 1]).astype(F32) for i in range(n)]
    return jnp.concatenate(rows, axis=0).astype(BF16)


def named_by(ids, e):
    return jnp.sum((ids == e.astype(F32)).astype(F32), axis=0, keepdims=True)


def earlier(n):
    rows = lax.broadcasted_iota(jnp.int32, (n, n), 0)
    return (rows < lax.broadcasted_iota(jnp.int32, (n, n), 1)).astype(F32).astype(BF16)


def dispatch(me, ids, cot, tokens, steps, groups, local, capacity):
    routes, part = cot.shape
    top_k, tok_rows = ids.shape
    width = tokens.shape[1]
    experts = groups * local
    step_rows = -(-3 * local // 8) * 8

    def kernel(me_ref, ids_ref, steps_ref, cot_hbm, tok_hbm, *refs):
        outs, own_ref, ids_out, steps_out = refs[:groups], *refs[groups : groups + 3]
        code_ref, cot_ref, sems = refs[groups + 3 :]
        cot_copy = pltpu.make_async_copy(cot_hbm, cot_ref, sems.at[0])
        tok_copy = pltpu.make_async_copy(tok_hbm, own_ref.at[:tok_rows, :], sems.at[1])
        cot_copy.start()
        tok_copy.start()
        step = steps_ref[...]
        high = step.astype(BF16).astype(F32)
        middle = (step - high).astype(BF16).astype(F32)
        low = step - high - middle
        thirds = [x[j : j + 1] for j in range(local) for x in (high, middle, low)]
        thirds += [jnp.zeros_like(thirds[0])] * (step_rows - 3 * local)
        steps_out[...] = jnp.concatenate(thirds, axis=0).astype(BF16)
        ids_t = ids_ref[...].astype(F32)
        ids_out[...] = ids_t
        own_ref[tok_rows:, :] = jnp.zeros((top_k, width), BF16)
        own_ref[tok_rows:, :tok_rows] = ids_t.astype(BF16)
        route = lax.broadcasted_iota(jnp.int32, (tok_rows, routes), 1)
        token = lax.broadcasted_iota(jnp.int32, (tok_rows, routes), 0)
        spread = jnp.dot(
            ids_t,
            (route // top_k == token).astype(F32),
            precision=lax.Precision.HIGHEST,
            preferred_element_type=F32,
        )
        choice = lax.broadcasted_iota(jnp.int32, (top_k, routes), 1) % top_k
        mask = choice == lax.broadcasted_iota(jnp.int32, (top_k, routes), 0)
        ids_row = jnp.sum(jnp.where(mask, spread, 0.0), axis=0, keepdims=True)
        ids_row = jnp.round(ids_row).astype(jnp.int32)
        expert = lax.broadcasted_iota(jnp.int32, (experts, routes), 0)
        named = expert == ids_row
        before = jnp.dot(named.astype(F32).astype(BF16), earlier(routes), preferred_element_type=F32)
        code_ref[...] = jnp.where(named, before.astype(jnp.int32), -1)
        slot = lax.broadcasted_iota(jnp.int32, (capacity, routes), 0)
        cot_copy.wait()
        for k in range(groups):
            for j in range(local):
                e = partner(k, me_ref[0], groups) * local + j
                pick = (slot == code_ref[pl.ds(e, 1), :]).astype(F32).astype(BF16)
                outs[k][j * capacity : (j + 1) * capacity, :] = jnp.dot(
                    pick, cot_ref[...], preferred_element_type=F32
                ).astype(BF16)
        tok_copy.wait()

    whole = lambda shape: pl.BlockSpec(shape, lambda i, me: (0, 0))
    return pl.pallas_call(
        kernel,
        grid_spec=pltpu.PrefetchScalarGridSpec(
            num_scalar_prefetch=1,
            grid=(1,),
            in_specs=[whole(ids.shape), whole(steps.shape)] + [pl.BlockSpec(memory_space=pltpu.HBM)] * 2,
            out_specs=[whole((local * capacity, part))] * groups
            + [whole((tok_rows + top_k, width)), whole((top_k, tok_rows)), whole((step_rows, part))],
            scratch_shapes=[
                pltpu.VMEM((experts, routes), jnp.int32),
                pltpu.VMEM(cot.shape, BF16),
                pltpu.SemaphoreType.DMA((2,)),
            ],
        ),
        out_shape=[jax.ShapeDtypeStruct((local * capacity, part), BF16)] * groups
        + [
            jax.ShapeDtypeStruct((tok_rows + top_k, width), BF16),
            jax.ShapeDtypeStruct((top_k, tok_rows), F32),
            jax.ShapeDtypeStruct((step_rows, part), BF16),
        ],
        compiler_params=params(),
        name="dispatch",
    )(
        me,
        ids,
        steps,
        pltpu.with_memory_space_constraint(cot, pltpu.HBM),
        pltpu.with_memory_space_constraint(tokens, pltpu.HBM),
    )


def expert_rows(me, blocks, groups, local, tok_rows, capacity):
    width = blocks[0].shape[1]
    dt = row_tile(width, 896)

    def kernel(me_ref, *refs):
        ids_refs, ins = refs[:groups], refs[groups : 2 * groups]
        outs, pick_ref = refs[2 * groups : -1], refs[-1]

        @pl.when(pl.program_id(0) == 0)
        def _():
            ids = [ids_refs[k][tok_rows:, :tok_rows].astype(F32) for k in range(groups)]
            member = [named_by(i, me_ref[0] * local + j) for j in range(local) for i in ids]
            pick_ref[...] = picks(jnp.concatenate(member, axis=0), capacity)

        for j in range(local):
            rows = jnp.concatenate(
                [
                    jnp.dot(pick_ref[pl.ds((j * groups + k) * capacity, capacity), :], ins[k][:tok_rows, :], preferred_element_type=F32)
                    for k in range(groups)
                ],
                axis=0,
            )
            outs[j][...] = rows.T.astype(BF16)

    rows_in = blocks[0].shape[0]
    return pl.pallas_call(
        kernel,
        grid_spec=pltpu.PrefetchScalarGridSpec(
            num_scalar_prefetch=1,
            grid=(width // dt,),
            in_specs=[pl.BlockSpec((rows_in, dt), lambda i, me: (0, 0))] * groups
            + [pl.BlockSpec((rows_in, dt), lambda i, me: (0, i))] * groups,
            out_specs=[pl.BlockSpec((dt, groups * capacity), lambda i, me: (i, 0))] * local,
            scratch_shapes=[pltpu.VMEM((local * groups * capacity, tok_rows), BF16)],
        ),
        out_shape=[jax.ShapeDtypeStruct((width, groups * capacity), BF16)] * local,
        compiler_params=params(),
        name="expert_rows",
    )(me, *blocks, *blocks)


def back_rows(chunks, quantized, capacity, counts):
    parts = sum(q.shape[0] for q in quantized)
    _, width, part = quantized[0].shape
    dt = row_tile(width, 896)
    flat = [g for arrays, _, _ in chunks for g in arrays]

    def kernel(*refs):
        q_refs = [r.at[n] for r in refs[len(flat) :][: len(quantized)] for n in range(r.shape[0])]
        total = None
        for r in range(parts):
            rows = jnp.concatenate([refs[n * parts + r][...] for n in range(len(chunks))], axis=0)
            term = lax.dot_general(
                rows, q_refs[r][...], (((1,), (1,)), ((), ())), preferred_element_type=F32
            )
            total = term if total is None else total + term
        at = 0
        for count, out in zip(counts, refs[len(flat) + len(quantized) :]):
            out[...] = total[at : at + count * capacity].astype(BF16)
            at += count * capacity

    return pl.pallas_call(
        kernel,
        grid=(width // dt,),
        in_specs=[
            pl.BlockSpec((rows, part), lambda i, block=block: (block, 0))
            for arrays, rows, block in chunks
            for _ in arrays
        ]
        + [pl.BlockSpec((q.shape[0], dt, part), lambda i: (0, i, 0)) for q in quantized],
        out_specs=[pl.BlockSpec((c * capacity, dt), lambda i: (0, i)) for c in counts],
        out_shape=[pltpu.HBM((c * capacity, width), BF16) for c in counts],
        compiler_params=params(),
        name="back_rows",
    )(*flat, *quantized)


def weight_part(mine, rows_t, chunks, slopes, step_slopes, j, shape, scale, before):
    parts = sum(a.shape[0] for a in slopes)
    _, width, part = slopes[0].shape
    dt = row_tile(width, 896)
    n_chunks = len(chunks)
    flat = [g for arrays, _, _ in chunks for g in arrays]
    held = 0 if before is None else 1

    def kernel(mine_ref, x_ref, *refs):
        gs = refs[: len(flat)]
        factors = refs[len(flat) :][: 2 * len(slopes)]
        factors = [r.at[n] for r in factors for n in range(r.shape[0])]
        sl, ts = factors[:parts], factors[parts:]
        out, st = refs[len(flat) + 2 * len(slopes) + held :]
        i = pl.program_id(0)
        for r in range(parts):
            raw, at = None, 0
            for n in range(n_chunks):
                g = gs[n * parts + r]
                size = g.shape[0]
                term = jnp.dot(x_ref[:, at : at + size], g[...], preferred_element_type=F32)
                raw = term if raw is None else raw + term
                at += size
            column = pl.multiple_of(partner(r, mine_ref[0], parts) * part, part)
            out[0, :, pl.ds(column, part)] = (raw * sl[r][...].astype(F32)).astype(BF16)
            sums = jnp.sum((raw * ts[r][...].astype(F32)).reshape(dt // 8, 8, part), axis=0) * scale
            st[r] = jnp.where(i == 0, sums, st[r] + sums)

    return pl.pallas_call(
        kernel,
        grid_spec=pltpu.PrefetchScalarGridSpec(
            num_scalar_prefetch=1,
            grid=(width // dt,),
            in_specs=[pl.BlockSpec((dt, rows_t.shape[1]), lambda i, m: (i, 0))]
            + [
                pl.BlockSpec((rows, part), lambda i, m, block=block: (block, 0))
                for arrays, rows, block in chunks
                for _ in arrays
            ]
            + [pl.BlockSpec((a.shape[0], dt, part), lambda i, m: (0, i, 0)) for a in slopes + step_slopes]
            + [pl.BlockSpec(memory_space=pl.ANY)] * held,
            out_specs=[
                pl.BlockSpec((1, dt, parts * part), lambda i, m: (j, i, 0)),
                pl.BlockSpec((parts, 8, part), lambda i, m: (0, 0, 0)),
            ],
        ),
        out_shape=[
            pltpu.HBM(shape, BF16),
            jax.ShapeDtypeStruct((parts, 8, part), F32),
        ],
        input_output_aliases={2 + len(flat) + 2 * len(slopes): 0} if held else {},
        compiler_params=params(),
        name="weight_part",
    )(mine, rows_t, *flat, *slopes, *step_slopes, *(() if before is None else (before,)))


def combine(me, ids_t, returned, groups, local, capacity):
    _, tok_rows = ids_t.shape
    names = [name for _, of_array in returned for name in of_array]
    width = returned[0][0].shape[1]
    dt = row_tile(width, 896)

    def kernel(me_ref, ids_ref, *refs):
        ins, out, pick_ref = refs[:-2], refs[-2], refs[-1]

        @pl.when(pl.program_id(0) == 0)
        def _():
            ids = ids_ref[...]
            member = [named_by(ids, partner(k, me_ref[0], groups) * local + j) for j, k in names]
            pick_ref[...] = picks(jnp.concatenate(member, axis=0), capacity)

        rows = jnp.concatenate([r[...] for r in ins], axis=0)
        out[...] = lax.dot_general(
            pick_ref[...], rows, (((0,), (0,)), ((), ())), preferred_element_type=F32
        ).astype(BF16)

    return pl.pallas_call(
        kernel,
        grid_spec=pltpu.PrefetchScalarGridSpec(
            num_scalar_prefetch=1,
            grid=(width // dt,),
            in_specs=[pl.BlockSpec(ids_t.shape, lambda i, me: (0, 0))]
            + [
                pl.BlockSpec((len(of_array) * capacity, dt), lambda i, me: (0, i))
                for _, of_array in returned
            ],
            out_specs=pl.BlockSpec((tok_rows, dt), lambda i, me: (0, i)),
            scratch_shapes=[pltpu.VMEM((len(names) * capacity, tok_rows), BF16)],
        ),
        out_shape=jax.ShapeDtypeStruct((tok_rows, width), BF16),
        compiler_params=params(),
        name="combine",
    )(me, ids_t, *[array for array, _ in returned])


def per_device(tokens, cotangent, weights, steps, expert_ids):
    groups, parts = lax.axis_size("expert"), lax.axis_size("mp")
    local = weights.shape[0]
    tok_rows, top_k = expert_ids.shape
    capacity = tok_rows // 2
    part = cotangent.shape[2]
    width = tokens.shape[1]
    me, mine = lax.axis_index("expert"), lax.axis_index("mp")
    me_arr = me.astype(jnp.int32)[None]
    mine_arr = mine.astype(jnp.int32)[None]
    expert_swap = lambda x, k: swap(x, "expert", k, groups)
    mp_swap = lambda x, r: swap(x, "mp", r, parts)
    spread = lambda x: [x] + [mp_swap(x, r) for r in range(1, parts)]

    *g_out, own, ids_t, thirds = dispatch(
        me_arr,
        expert_ids.T,
        cotangent.reshape(tok_rows * top_k, part),
        tokens,
        steps,
        groups,
        local,
        capacity,
    )
    near_in = expert_swap(g_out[1], 1)
    g_in = [g_out[0], near_in] + [expert_swap(g_out[k], k) for k in range(2, groups)]
    of = lambda j, k: g_in[k][j * capacity : (j + 1) * capacity]
    near = [0, 1]
    first = spread(jnp.concatenate([of(j, k) for j in range(local) for k in near] + [thirds], axis=0))
    far = {}
    for j in range(local):
        ks = list(range(2, groups))
        if ks:
            rows = jnp.concatenate([of(j, k) for k in ks], axis=0)
            far[j] = [(ks, (spread(rows), rows.shape[0], 0))]
    blocks = [own] + [None] * (groups - 1)
    for k in range(2, groups, 2):
        blocks[k] = expert_swap(own, k)
    for k in range(1, groups, 2):
        blocks[k] = expert_swap(blocks[k - 1], 1)

    pieces = [[] for _ in range(local)]
    at = local * len(near) * capacity
    for low, high in [(0, 1), (1, parts)] if parts > 1 else [(0, 1)]:
        for j in range(local):
            pieces[j].append(quantize(mine_arr, weights, first, at, j, low, high))
    quantized = [[list(a) for a in zip(*of_expert)] for of_expert in pieces]
    rows_t = expert_rows(me_arr, blocks, groups, local, tok_rows, capacity)

    returned, weight_out, partial = [], None, []
    scale = QMAX / math.sqrt(width * parts * QMAX)
    for j in range(local):
        values, slopes, step_slopes = quantized[j]
        chunks = [(near, (first, len(near) * capacity, j))] + far.get(j, [])
        ks = [k for of_chunk, _ in chunks for k in of_chunk]
        outs = back_rows([c for _, c in chunks], values, capacity, [1] * len(ks))
        for k, rows in zip(ks, outs):
            returned.append((rows if k == 0 else expert_swap(rows, k), [(j, k)]))
        weight_out, sums = weight_part(
            mine_arr,
            rows_t[j],
            [c for _, c in chunks],
            slopes,
            step_slopes,
            j,
            weights.shape,
            scale,
            weight_out,
        )
        partial.append(sums)
    sums = jnp.stack([p.sum(axis=1) for p in partial], axis=1)
    others = [mp_swap(sums[r], r) for r in range(1, parts)]
    step_out = sum(others, sums[0])
    token_out = combine(me_arr, ids_t, returned, groups, local, capacity)
    return (token_out, weight_out, step_out)


def solution(mesh):
    return jax.shard_map(
        per_device,
        mesh=mesh,
        in_specs=(
            P("expert", "mp"),
            P("expert", None, "mp"),
            P("expert", "mp", None),
            P("expert", "mp"),
            P("expert", None),
        ),
        out_specs=(P("expert", "mp"), P("expert", "mp", None), P("expert", "mp")),
        check_vma=False,
    )
```

```python
import math

import jax
import jax.numpy as jnp
from jax import lax
from jax.experimental import pallas as pl
from jax.experimental.pallas import tpu as pltpu
from jax.sharding import PartitionSpec as P


QMAX = 7.0
WIGGLE = 0.9
BF16 = jnp.bfloat16
F32 = jnp.float32

SIN = (3.1415820221481474, -5.167142796288472, 2.5418990269458197, -0.5546361956218614)
SCALED = tuple(math.sqrt(2.0 * WIGGLE) * k for k in SIN)
ROUNDER = 12582912.0


def params(mib=48):
    return pltpu.CompilerParams(vmem_limit_bytes=mib * 1024 * 1024)


def partner(offset, index, size):
    if size & (size - 1) == 0:
        return index ^ offset
    return (offset - index) % size


def swap(x, axis, offset, size):
    return lax.ppermute(x, axis, [(i, partner(offset, i, size)) for i in range(size)])


def row_tile(rows, want):
    tile = min(rows, want)
    while rows % tile:
        tile //= 2
    return tile


def quantize(mine, weights, steps, at, j, low, high):
    parts = len(steps)
    rows_in = -(-3 * weights.shape[0] // 8) * 8
    _, width, full = weights.shape
    part = full // parts
    dt = row_tile(width, 896)
    chunk = row_tile(dt, 16)

    def kernel(mine_ref, w_ref, *refs):
        q_ref, sl_ref, ts_ref = refs[high - low :]
        thirds = refs[0][...].astype(F32)
        for r in range(1, high - low):
            thirds = jnp.where(pl.program_id(0) == r, refs[r][...].astype(F32), thirds)
        step = thirds[3 * j : 3 * j + 1] + thirds[3 * j + 1 : 3 * j + 2] + thirds[3 * j + 2 : 3 * j + 3]
        inv = 1.0 / (QMAX * step)
        step7 = QMAX * step

        def body(i, carry):
            rows = pl.ds(pl.multiple_of(i * chunk, chunk), chunk)
            t = w_ref[0, rows, :].astype(F32) * inv
            u = jnp.tanh(t)
            c = QMAX * u
            r = c - ((c + ROUNDER) - ROUNDER)
            y = r * r
            poly = SCALED[-1]
            for k in SCALED[-2::-1]:
                poly = poly * y + k
            sine = r * poly
            z = sine * sine
            x = 2.0 * WIGGLE * 1.0000005 - z
            cosine = x * lax.rsqrt(x)
            level = u - (0.5 / (math.pi * QMAX)) * (sine * cosine)
            slopes = (1.0 - WIGGLE + z) * (1.0 - u * u)
            q_ref[0, rows, :] = (step7 * level).astype(BF16)
            sl_ref[0, rows, :] = slopes.astype(BF16)
            ts_ref[0, rows, :] = (level - t * slopes).astype(BF16)
            return carry

        lax.fori_loop(0, dt // chunk, body, 0, unroll=2 if dt // chunk % 2 == 0 else 1)

    return pl.pallas_call(
        kernel,
        grid_spec=pltpu.PrefetchScalarGridSpec(
            num_scalar_prefetch=1,
            grid=(high - low, width // dt),
            in_specs=[
                pl.BlockSpec((1, dt, part), lambda r, i, mine: (j, i, partner(r + low, mine[0], parts))),
            ]
            + [pl.BlockSpec((rows_in, part), lambda r, i, mine: (at // rows_in, 0))] * (high - low),
            out_specs=[pl.BlockSpec((1, dt, part), lambda r, i, mine: (r, i, 0))] * 3,
        ),
        out_shape=[pltpu.HBM((high - low, width, part), BF16)] * 3,
        compiler_params=params(),
        name="quantize",
    )(mine, weights, *steps[low:high])


def picks(member, capacity):
    n, tok_rows = member.shape
    before = jnp.dot(member.astype(BF16), earlier(tok_rows), preferred_element_type=F32)
    code = jnp.where(member > 0.5, before, -1.0).astype(jnp.int32)
    slot = lax.broadcasted_iota(jnp.int32, (capacity, tok_rows), 0)
    rows = [(slot == code[i : i + 1]).astype(F32) for i in range(n)]
    return jnp.concatenate(rows, axis=0).astype(BF16)


def named_by(ids, e):
    return jnp.sum((ids == e.astype(F32)).astype(F32), axis=0, keepdims=True)


def earlier(n):
    rows = lax.broadcasted_iota(jnp.int32, (n, n), 0)
    return (rows < lax.broadcasted_iota(jnp.int32, (n, n), 1)).astype(F32).astype(BF16)


def dispatch(me, ids, cot, tokens, steps, groups, local, capacity):
    routes, part = cot.shape
    top_k, tok_rows = ids.shape
    width = tokens.shape[1]
    experts = groups * local
    step_rows = -(-3 * local // 8) * 8

    def kernel(me_ref, ids_hbm, steps_hbm, cot_hbm, tok_hbm, *refs):
        outs, own_ref, ids_out, steps_out = refs[:groups], *refs[groups : groups + 3]
        code_ref, ids_ref, steps_ref, cot_ref, sems = refs[groups + 3 :]
        ids_copy = pltpu.make_async_copy(ids_hbm, ids_ref, sems.at[2])
        steps_copy = pltpu.make_async_copy(steps_hbm, steps_ref, sems.at[3])
        ids_copy.start()
        steps_copy.start()
        cot_copy = pltpu.make_async_copy(cot_hbm, cot_ref, sems.at[0])
        tok_copy = pltpu.make_async_copy(tok_hbm, own_ref.at[:tok_rows, :], sems.at[1])
        cot_copy.start()
        tok_copy.start()
        ids_copy.wait()
        steps_copy.wait()
        step = steps_ref[...]
        high = step.astype(BF16).astype(F32)
        middle = (step - high).astype(BF16).astype(F32)
        low = step - high - middle
        thirds = [x[j : j + 1] for j in range(local) for x in (high, middle, low)]
        thirds += [jnp.zeros_like(thirds[0])] * (step_rows - 3 * local)
        steps_out[...] = jnp.concatenate(thirds, axis=0).astype(BF16)
        ids_t = ids_ref[...].astype(F32)
        ids_out[...] = ids_t
        own_ref[tok_rows:, :] = jnp.zeros((top_k, width), BF16)
        own_ref[tok_rows:, :tok_rows] = ids_t.astype(BF16)
        route = lax.broadcasted_iota(jnp.int32, (tok_rows, routes), 1)
        token = lax.broadcasted_iota(jnp.int32, (tok_rows, routes), 0)
        spread = jnp.dot(
            ids_t,
            (route // top_k == token).astype(F32),
            precision=lax.Precision.HIGHEST,
            preferred_element_type=F32,
        )
        choice = lax.broadcasted_iota(jnp.int32, (top_k, routes), 1) % top_k
        mask = choice == lax.broadcasted_iota(jnp.int32, (top_k, routes), 0)
        ids_row = jnp.sum(jnp.where(mask, spread, 0.0), axis=0, keepdims=True)
        ids_row = jnp.round(ids_row).astype(jnp.int32)
        expert = lax.broadcasted_iota(jnp.int32, (experts, routes), 0)
        named = expert == ids_row
        before = jnp.dot(named.astype(F32).astype(BF16), earlier(routes), preferred_element_type=F32)
        code_ref[...] = jnp.where(named, before.astype(jnp.int32), -1)
        slot = lax.broadcasted_iota(jnp.int32, (capacity, routes), 0)
        cot_copy.wait()
        size = local * capacity
        for low in range(0, groups, 4):
            ks = range(low, min(low + 4, groups))
            codes = [
                code_ref[pl.ds(partner(k, me_ref[0], groups) * local + j, 1), :]
                for k in ks
                for j in range(local)
            ]
            pick = jnp.concatenate([(slot == code).astype(F32) for code in codes], axis=0)
            rows = jnp.dot(pick.astype(BF16), cot_ref[...], preferred_element_type=F32).astype(BF16)
            for n, k in enumerate(ks):
                outs[k][...] = rows[n * size : (n + 1) * size]
        tok_copy.wait()

    whole = lambda shape: pl.BlockSpec(shape, lambda i, me: (0, 0))
    return pl.pallas_call(
        kernel,
        grid_spec=pltpu.PrefetchScalarGridSpec(
            num_scalar_prefetch=1,
            grid=(1,),
            in_specs=[pl.BlockSpec(memory_space=pltpu.HBM)] * 4,
            out_specs=[whole((local * capacity, part))] * groups
            + [whole((tok_rows + top_k, width)), whole((top_k, tok_rows)), whole((step_rows, part))],
            scratch_shapes=[
                pltpu.VMEM((experts, routes), jnp.int32),
                pltpu.VMEM(ids.shape, jnp.int32),
                pltpu.VMEM(steps.shape, F32),
                pltpu.VMEM(cot.shape, BF16),
                pltpu.SemaphoreType.DMA((4,)),
            ],
        ),
        out_shape=[jax.ShapeDtypeStruct((local * capacity, part), BF16)] * groups
        + [
            jax.ShapeDtypeStruct((tok_rows + top_k, width), BF16),
            jax.ShapeDtypeStruct((top_k, tok_rows), F32),
            jax.ShapeDtypeStruct((step_rows, part), BF16),
        ],
        compiler_params=params(),
        name="dispatch",
    )(
        me,
        *[pltpu.with_memory_space_constraint(x, pltpu.HBM) for x in (ids, steps, cot, tokens)],
    )


def expert_rows(me, blocks, groups, local, tok_rows, capacity):
    width = blocks[0].shape[1]
    dt = row_tile(width, 896)

    def kernel(me_ref, *refs):
        ids_refs, ins = refs[:groups], refs[groups : 2 * groups]
        outs, pick_ref = refs[2 * groups : -1], refs[-1]

        @pl.when(pl.program_id(0) == 0)
        def _():
            ids = [ids_refs[k][tok_rows:, :tok_rows].astype(F32) for k in range(groups)]
            member = [named_by(i, me_ref[0] * local + j) for i in ids for j in range(local)]
            pick_ref[...] = picks(jnp.concatenate(member, axis=0), capacity)

        size = local * capacity
        rows = [
            jnp.dot(
                pick_ref[k * size : (k + 1) * size, :],
                ins[k][:tok_rows, :],
                preferred_element_type=F32,
            )
            for k in range(groups)
        ]
        for j in range(local):
            of_expert = [r[j * capacity : (j + 1) * capacity] for r in rows]
            outs[j][...] = jnp.concatenate(of_expert, axis=0).T.astype(BF16)

    rows_in = blocks[0].shape[0]
    return pl.pallas_call(
        kernel,
        grid_spec=pltpu.PrefetchScalarGridSpec(
            num_scalar_prefetch=1,
            grid=(width // dt,),
            in_specs=[pl.BlockSpec((rows_in, dt), lambda i, me: (0, 0))] * groups
            + [pl.BlockSpec((rows_in, dt), lambda i, me: (0, i))] * groups,
            out_specs=[pl.BlockSpec((dt, groups * capacity), lambda i, me: (i, 0))] * local,
            scratch_shapes=[pltpu.VMEM((local * groups * capacity, tok_rows), BF16)],
        ),
        out_shape=[jax.ShapeDtypeStruct((width, groups * capacity), BF16)] * local,
        compiler_params=params(),
        name="expert_rows",
    )(me, *blocks, *blocks)


def back_rows(chunks, quantized, capacity, counts):
    parts = sum(q.shape[0] for q in quantized)
    _, width, part = quantized[0].shape
    dt = row_tile(width, 896)
    flat = [g for arrays, _, _ in chunks for g in arrays]

    def kernel(*refs):
        q_refs = [r.at[n] for r in refs[len(flat) :][: len(quantized)] for n in range(r.shape[0])]
        total = None
        for r in range(parts):
            rows = jnp.concatenate([refs[n * parts + r][...] for n in range(len(chunks))], axis=0)
            term = lax.dot_general(
                q_refs[r][...], rows, (((1,), (1,)), ((), ())), preferred_element_type=F32
            )
            total = term if total is None else total + term
        total = total.T
        at = 0
        for count, out in zip(counts, refs[len(flat) + len(quantized) :]):
            out[...] = total[at : at + count * capacity].astype(BF16)
            at += count * capacity

    return pl.pallas_call(
        kernel,
        grid=(width // dt,),
        in_specs=[
            pl.BlockSpec((rows, part), lambda i, block=block: (block, 0))
            for arrays, rows, block in chunks
            for _ in arrays
        ]
        + [pl.BlockSpec((q.shape[0], dt, part), lambda i: (0, i, 0)) for q in quantized],
        out_specs=[pl.BlockSpec((c * capacity, dt), lambda i: (0, i)) for c in counts],
        out_shape=[pltpu.HBM((c * capacity, width), BF16) for c in counts],
        compiler_params=params(),
        name="back_rows",
    )(*flat, *quantized)


def weight_part(mine, rows_t, chunks, slopes, step_slopes, j, shape, scale, before):
    parts = sum(a.shape[0] for a in slopes)
    _, width, part = slopes[0].shape
    dt = row_tile(width, 896)
    n_chunks = len(chunks)
    flat = [g for arrays, _, _ in chunks for g in arrays]
    held = 0 if before is None else 1

    def kernel(mine_ref, x_ref, *refs):
        gs = refs[: len(flat)]
        factors = refs[len(flat) :][: 2 * len(slopes)]
        factors = [r.at[n] for r in factors for n in range(r.shape[0])]
        sl, ts = factors[:parts], factors[parts:]
        out, st = refs[len(flat) + 2 * len(slopes) + held :]
        i = pl.program_id(0)
        for r in range(parts):
            g = jnp.concatenate([gs[n * parts + r][...] for n in range(n_chunks)], axis=0)
            raw = jnp.dot(x_ref[...], g, preferred_element_type=F32)
            column = pl.multiple_of(partner(r, mine_ref[0], parts) * part, part)
            out[0, :, pl.ds(column, part)] = (raw * sl[r][...].astype(F32)).astype(BF16)
            sums = jnp.sum((raw * ts[r][...].astype(F32)).reshape(dt // 8, 8, part), axis=0) * scale
            st[r] = jnp.where(i == 0, sums, st[r] + sums)

    return pl.pallas_call(
        kernel,
        grid_spec=pltpu.PrefetchScalarGridSpec(
            num_scalar_prefetch=1,
            grid=(width // dt,),
            in_specs=[pl.BlockSpec((dt, rows_t.shape[1]), lambda i, m: (i, 0))]
            + [
                pl.BlockSpec((rows, part), lambda i, m, block=block: (block, 0))
                for arrays, rows, block in chunks
                for _ in arrays
            ]
            + [pl.BlockSpec((a.shape[0], dt, part), lambda i, m: (0, i, 0)) for a in slopes + step_slopes]
            + [pl.BlockSpec(memory_space=pl.ANY)] * held,
            out_specs=[
                pl.BlockSpec((1, dt, parts * part), lambda i, m: (j, i, 0)),
                pl.BlockSpec((parts, 8, part), lambda i, m: (0, 0, 0)),
            ],
        ),
        out_shape=[
            pltpu.HBM(shape, BF16),
            jax.ShapeDtypeStruct((parts, 8, part), F32),
        ],
        input_output_aliases={2 + len(flat) + 2 * len(slopes): 0} if held else {},
        compiler_params=params(),
        name="weight_part",
    )(mine, rows_t, *flat, *slopes, *step_slopes, *(() if before is None else (before,)))


def combine(me, ids_t, returned, groups, local, capacity):
    _, tok_rows = ids_t.shape
    names = [name for _, of_array in returned for name in of_array]
    width = returned[0][0].shape[1]
    dt = row_tile(width, 896)

    def kernel(me_ref, ids_ref, *refs):
        ins, out, pick_ref = refs[:-2], refs[-2], refs[-1]

        @pl.when(pl.program_id(0) == 0)
        def _():
            ids = ids_ref[...]
            member = [named_by(ids, partner(k, me_ref[0], groups) * local + j) for j, k in names]
            pick_ref[...] = picks(jnp.concatenate(member, axis=0), capacity)

        rows = jnp.concatenate([r[...] for r in ins], axis=0)
        out[...] = lax.dot_general(
            pick_ref[...], rows, (((0,), (0,)), ((), ())), preferred_element_type=F32
        ).astype(BF16)

    return pl.pallas_call(
        kernel,
        grid_spec=pltpu.PrefetchScalarGridSpec(
            num_scalar_prefetch=1,
            grid=(width // dt,),
            in_specs=[pl.BlockSpec(ids_t.shape, lambda i, me: (0, 0))]
            + [
                pl.BlockSpec((len(of_array) * capacity, dt), lambda i, me: (0, i))
                for _, of_array in returned
            ],
            out_specs=pl.BlockSpec((tok_rows, dt), lambda i, me: (0, i)),
            scratch_shapes=[pltpu.VMEM((len(names) * capacity, tok_rows), BF16)],
        ),
        out_shape=jax.ShapeDtypeStruct((tok_rows, width), BF16),
        compiler_params=params(),
        name="combine",
    )(me, ids_t, *[array for array, _ in returned])


def per_device(tokens, cotangent, weights, steps, expert_ids):
    groups, parts = lax.axis_size("expert"), lax.axis_size("mp")
    local = weights.shape[0]
    tok_rows, top_k = expert_ids.shape
    capacity = tok_rows // 2
    part = cotangent.shape[2]
    width = tokens.shape[1]
    me, mine = lax.axis_index("expert"), lax.axis_index("mp")
    me_arr = me.astype(jnp.int32)[None]
    mine_arr = mine.astype(jnp.int32)[None]
    expert_swap = lambda x, k: swap(x, "expert", k, groups)
    mp_swap = lambda x, r: swap(x, "mp", r, parts)
    spread = lambda x: [x] + [mp_swap(x, r) for r in range(1, parts)]

    *g_out, own, ids_t, thirds = dispatch(
        me_arr,
        expert_ids.T,
        cotangent.reshape(tok_rows * top_k, part),
        tokens,
        steps,
        groups,
        local,
        capacity,
    )
    near_in = expert_swap(g_out[1], 1)
    g_in = [g_out[0], near_in] + [expert_swap(g_out[k], k) for k in range(2, groups)]
    of = lambda j, k: g_in[k][j * capacity : (j + 1) * capacity]
    near = [0, 1]
    first = spread(jnp.concatenate([of(j, k) for j in range(local) for k in near] + [thirds], axis=0))
    far = {}
    for j in range(local):
        ks = list(range(2, groups))
        if ks:
            rows = jnp.concatenate([of(j, k) for k in ks], axis=0)
            far[j] = [(ks, (spread(rows), rows.shape[0], 0))]
    blocks = [own] + [None] * (groups - 1)
    for k in range(2, groups, 2):
        blocks[k] = expert_swap(own, k)
    for k in range(1, groups, 2):
        blocks[k] = expert_swap(blocks[k - 1], 1)

    pieces = [[] for _ in range(local)]
    at = local * len(near) * capacity
    for j in range(local):
        cuts = [0, 1, parts] if j == 0 else [0, parts // 2, parts]
        for low, high in zip(cuts, cuts[1:]):
            if low < high:
                pieces[j].append(quantize(mine_arr, weights, first, at, j, low, high))
    quantized = [[list(a) for a in zip(*of_expert)] for of_expert in pieces]
    rows_t = expert_rows(me_arr, blocks, groups, local, tok_rows, capacity)

    returned, weight_out, partial = [], None, []
    scale = QMAX / math.sqrt(width * parts * QMAX)
    for j in range(local):
        values, slopes, step_slopes = quantized[j]
        chunks = [(near, (first, len(near) * capacity, j))] + far.get(j, [])
        ks = [k for of_chunk, _ in chunks for k in of_chunk]
        outs = back_rows([c for _, c in chunks], values, capacity, [1] * len(ks))
        for k, rows in zip(ks, outs):
            returned.append((rows if k == 0 else expert_swap(rows, k), [(j, k)]))
        weight_out, sums = weight_part(
            mine_arr,
            rows_t[j],
            [c for _, c in chunks],
            slopes,
            step_slopes,
            j,
            weights.shape,
            scale,
            weight_out,
        )
        partial.append(sums)
    sums = jnp.stack([p.sum(axis=1) for p in partial], axis=1)
    others = [mp_swap(sums[r], r) for r in range(1, parts)]
    step_out = sum(others, sums[0])
    token_out = combine(me_arr, ids_t, returned, groups, local, capacity)
    return (token_out, weight_out, step_out)


def solution(mesh):
    return jax.shard_map(
        per_device,
        mesh=mesh,
        in_specs=(
            P("expert", "mp"),
            P("expert", None, "mp"),
            P("expert", "mp", None),
            P("expert", "mp"),
            P("expert", None),
        ),
        out_specs=(P("expert", "mp"), P("expert", "mp", None), P("expert", "mp")),
        check_vma=False,
    )
```

```python
import math

import jax
import jax.numpy as jnp
from jax import lax
from jax.experimental import pallas as pl
from jax.experimental.pallas import tpu as pltpu
from jax.sharding import PartitionSpec as P


QMAX = 7.0
WIGGLE = 0.9
BF16 = jnp.bfloat16
F32 = jnp.float32

SIN = (3.1415820221481474, -5.167142796288472, 2.5418990269458197, -0.5546361956218614)
SCALED = tuple(math.sqrt(2.0 * WIGGLE) * k for k in SIN)
ROUNDER = 12582912.0


def params(mib=48):
    return pltpu.CompilerParams(vmem_limit_bytes=mib * 1024 * 1024)


def in_hbm(x):
    return pltpu.with_memory_space_constraint(x, pltpu.HBM)


def partner(offset, index, size):
    if size & (size - 1) == 0:
        return index ^ offset
    return (offset - index) % size


def swap(x, axis, offset, size):
    return lax.ppermute(x, axis, [(i, partner(offset, i, size)) for i in range(size)])


def spread(x, parts, relay):
    if not relay:
        return [(x,)] + [(swap(x, "mp", r, parts),) for r in range(1, parts)]
    two = swap(x, "mp", 2, parts)
    one = swap(x, "mp", 1, parts)
    inner = lax.ppermute(x, "mp", [(1, 2), (2, 1)])
    outer = lax.ppermute(two, "mp", [(1, 0), (2, 3)])
    return [(x,), (one,), (two,), (inner, outer)]


def total_of(refs):
    value = refs[0][...]
    for ref in refs[1:]:
        value = value + ref[...]
    return value


def grouped(refs, sizes):
    out, at = [], 0
    for size in sizes:
        out.append(list(refs[at : at + size]))
        at += size
    return out


def row_tile(rows, want):
    tile = min(rows, want)
    while rows % tile:
        tile //= 2
    return tile


def quantize(mine, weights, steps, at, j, low, high):
    parts = len(steps)
    rows_in = -(-3 * weights.shape[0] // 8) * 8
    _, width, full = weights.shape
    part = full // parts
    dt = row_tile(width, 896)
    chunk = row_tile(dt, 16)

    def kernel(mine_ref, w_ref, *refs):
        q_ref, sl_ref, ts_ref = refs[high - low :]
        thirds = refs[0][...].astype(F32)
        for r in range(1, high - low):
            thirds = jnp.where(pl.program_id(0) == r, refs[r][...].astype(F32), thirds)
        step = thirds[3 * j : 3 * j + 1] + thirds[3 * j + 1 : 3 * j + 2] + thirds[3 * j + 2 : 3 * j + 3]
        inv = 1.0 / (QMAX * step)
        step7 = QMAX * step

        def body(i, carry):
            rows = pl.ds(pl.multiple_of(i * chunk, chunk), chunk)
            t = w_ref[0, rows, :].astype(F32) * inv
            u = jnp.tanh(t)
            c = QMAX * u
            r = c - ((c + ROUNDER) - ROUNDER)
            y = r * r
            poly = SCALED[-1]
            for k in SCALED[-2::-1]:
                poly = poly * y + k
            sine = r * poly
            z = sine * sine
            x = 2.0 * WIGGLE * 1.0000005 - z
            cosine = x * lax.rsqrt(x)
            level = u - (0.5 / (math.pi * QMAX)) * (sine * cosine)
            slopes = (1.0 - WIGGLE + z) * (1.0 - u * u)
            q_ref[0, rows, :] = (step7 * level).astype(BF16)
            sl_ref[0, rows, :] = slopes.astype(BF16)
            ts_ref[0, rows, :] = (level - t * slopes).astype(BF16)
            return carry

        lax.fori_loop(0, dt // chunk, body, 0, unroll=2 if dt // chunk % 2 == 0 else 1)

    return pl.pallas_call(
        kernel,
        grid_spec=pltpu.PrefetchScalarGridSpec(
            num_scalar_prefetch=1,
            grid=(high - low, width // dt),
            in_specs=[
                pl.BlockSpec((1, dt, part), lambda r, i, mine: (j, i, partner(r + low, mine[0], parts))),
            ]
            + [pl.BlockSpec((rows_in, part), lambda r, i, mine: (at // rows_in, 0))] * (high - low),
            out_specs=[pl.BlockSpec((1, dt, part), lambda r, i, mine: (r, i, 0))] * 3,
        ),
        out_shape=[pltpu.HBM((high - low, width, part), BF16)] * 3,
        compiler_params=params(),
        name="quantize",
    )(mine, weights, *steps[low:high])


def picks(member, capacity):
    n, tok_rows = member.shape
    before = jnp.dot(member.astype(BF16), earlier(tok_rows), preferred_element_type=F32)
    code = jnp.where(member > 0.5, before, -1.0).astype(jnp.int32)
    slot = lax.broadcasted_iota(jnp.int32, (capacity, tok_rows), 0)
    rows = [(slot == code[i : i + 1]).astype(F32) for i in range(n)]
    return jnp.concatenate(rows, axis=0).astype(BF16)


def named_by(ids, e):
    return jnp.sum((ids == e.astype(F32)).astype(F32), axis=0, keepdims=True)


def earlier(n):
    rows = lax.broadcasted_iota(jnp.int32, (n, n), 0)
    return (rows < lax.broadcasted_iota(jnp.int32, (n, n), 1)).astype(F32).astype(BF16)


def dispatch(me, ids, cot, tokens, steps, groups, local, capacity):
    routes, part = cot.shape
    top_k, tok_rows = ids.shape
    width = tokens.shape[1]
    experts = groups * local
    step_rows = -(-3 * local // 8) * 8

    def kernel(me_ref, ids_hbm, steps_hbm, cot_hbm, tok_hbm, *refs):
        outs, own_ref, ids_out, steps_out = refs[:groups], *refs[groups : groups + 3]
        code_ref, ids_ref, steps_ref, cot_ref, sems = refs[groups + 3 :]
        ids_copy = pltpu.make_async_copy(ids_hbm, ids_ref, sems.at[2])
        steps_copy = pltpu.make_async_copy(steps_hbm, steps_ref, sems.at[3])
        ids_copy.start()
        steps_copy.start()
        cot_copy = pltpu.make_async_copy(cot_hbm, cot_ref, sems.at[0])
        tok_copy = pltpu.make_async_copy(tok_hbm, own_ref.at[:tok_rows, :], sems.at[1])
        cot_copy.start()
        tok_copy.start()
        ids_copy.wait()
        steps_copy.wait()
        step = steps_ref[...]
        high = step.astype(BF16).astype(F32)
        middle = (step - high).astype(BF16).astype(F32)
        low = step - high - middle
        thirds = [x[j : j + 1] for j in range(local) for x in (high, middle, low)]
        thirds += [jnp.zeros_like(thirds[0])] * (step_rows - 3 * local)
        steps_out[...] = jnp.concatenate(thirds, axis=0).astype(BF16)
        ids_t = ids_ref[...].astype(F32)
        ids_out[...] = ids_t
        own_ref[tok_rows:, :] = jnp.zeros((top_k, width), BF16)
        own_ref[tok_rows:, :tok_rows] = ids_t.astype(BF16)
        route = lax.broadcasted_iota(jnp.int32, (tok_rows, routes), 1)
        token = lax.broadcasted_iota(jnp.int32, (tok_rows, routes), 0)
        spread = jnp.dot(
            ids_t,
            (route // top_k == token).astype(F32),
            precision=lax.Precision.HIGHEST,
            preferred_element_type=F32,
        )
        choice = lax.broadcasted_iota(jnp.int32, (top_k, routes), 1) % top_k
        mask = choice == lax.broadcasted_iota(jnp.int32, (top_k, routes), 0)
        ids_row = jnp.sum(jnp.where(mask, spread, 0.0), axis=0, keepdims=True)
        ids_row = jnp.round(ids_row).astype(jnp.int32)
        expert = lax.broadcasted_iota(jnp.int32, (experts, routes), 0)
        named = expert == ids_row
        before = jnp.dot(named.astype(F32).astype(BF16), earlier(routes), preferred_element_type=F32)
        code_ref[...] = jnp.where(named, before.astype(jnp.int32), -1)
        slot = lax.broadcasted_iota(jnp.int32, (capacity, routes), 0)
        cot_copy.wait()
        size = local * capacity
        for low in range(0, groups, 4):
            ks = range(low, min(low + 4, groups))
            codes = [
                code_ref[pl.ds(partner(k, me_ref[0], groups) * local + j, 1), :]
                for k in ks
                for j in range(local)
            ]
            pick = jnp.concatenate([(slot == code).astype(F32) for code in codes], axis=0)
            rows = jnp.dot(pick.astype(BF16), cot_ref[...], preferred_element_type=F32).astype(BF16)
            for n, k in enumerate(ks):
                outs[k][...] = rows[n * size : (n + 1) * size]
        tok_copy.wait()

    whole = lambda shape: pl.BlockSpec(shape, lambda i, me: (0, 0))
    return pl.pallas_call(
        kernel,
        grid_spec=pltpu.PrefetchScalarGridSpec(
            num_scalar_prefetch=1,
            grid=(1,),
            in_specs=[pl.BlockSpec(memory_space=pltpu.HBM)] * 4,
            out_specs=[whole((local * capacity, part))] * groups
            + [whole((tok_rows + top_k, width)), whole((top_k, tok_rows)), whole((step_rows, part))],
            scratch_shapes=[
                pltpu.VMEM((experts, routes), jnp.int32),
                pltpu.VMEM(ids.shape, jnp.int32),
                pltpu.VMEM(steps.shape, F32),
                pltpu.VMEM(cot.shape, BF16),
                pltpu.SemaphoreType.DMA((4,)),
            ],
        ),
        out_shape=[jax.ShapeDtypeStruct((local * capacity, part), BF16)] * groups
        + [
            jax.ShapeDtypeStruct((tok_rows + top_k, width), BF16),
            jax.ShapeDtypeStruct((top_k, tok_rows), F32),
            jax.ShapeDtypeStruct((step_rows, part), BF16),
        ],
        compiler_params=params(),
        name="dispatch",
    )(
        me,
        *[in_hbm(x) for x in (ids, steps, cot, tokens)],
    )


def expert_rows(me, blocks, groups, local, tok_rows, capacity):
    width = blocks[0].shape[1]
    dt = row_tile(width, 896)

    def kernel(me_ref, *refs):
        ids_refs, ins = refs[:groups], refs[groups : 2 * groups]
        outs, pick_ref = refs[2 * groups : -1], refs[-1]

        @pl.when(pl.program_id(0) == 0)
        def _():
            ids = [ids_refs[k][tok_rows:, :tok_rows].astype(F32) for k in range(groups)]
            member = [named_by(i, me_ref[0] * local + j) for i in ids for j in range(local)]
            pick_ref[...] = picks(jnp.concatenate(member, axis=0), capacity)

        size = local * capacity
        rows = [
            jnp.dot(
                pick_ref[k * size : (k + 1) * size, :],
                ins[k][:tok_rows, :],
                preferred_element_type=F32,
            )
            for k in range(groups)
        ]
        for j in range(local):
            of_expert = [r[j * capacity : (j + 1) * capacity] for r in rows]
            outs[j][...] = jnp.concatenate(of_expert, axis=0).T.astype(BF16)

    rows_in = blocks[0].shape[0]
    return pl.pallas_call(
        kernel,
        grid_spec=pltpu.PrefetchScalarGridSpec(
            num_scalar_prefetch=1,
            grid=(width // dt,),
            in_specs=[pl.BlockSpec((rows_in, dt), lambda i, me: (0, 0))] * groups
            + [pl.BlockSpec((rows_in, dt), lambda i, me: (0, i))] * groups,
            out_specs=[pl.BlockSpec((dt, groups * capacity), lambda i, me: (i, 0))] * local,
            scratch_shapes=[pltpu.VMEM((local * groups * capacity, tok_rows), BF16)],
        ),
        out_shape=[pltpu.HBM((width, groups * capacity), BF16)] * local,
        compiler_params=params(),
        name="expert_rows",
    )(me, *blocks, *blocks)


def back_rows(chunks, quantized, capacity, counts):
    parts = sum(q.shape[0] for q in quantized)
    _, width, part = quantized[0].shape
    dt = row_tile(width, 896)
    flat = [g for arrays, _, _ in chunks for of_part in arrays for g in of_part]
    sizes = [len(of_part) for arrays, _, _ in chunks for of_part in arrays]

    def kernel(*refs):
        q_refs = [r.at[n] for r in refs[len(flat) :][: len(quantized)] for n in range(r.shape[0])]
        gs = grouped(refs, sizes)
        total = None
        for r in range(parts):
            rows = jnp.concatenate([total_of(gs[n * parts + r]) for n in range(len(chunks))], axis=0)
            term = lax.dot_general(
                q_refs[r][...], rows, (((1,), (1,)), ((), ())), preferred_element_type=F32
            )
            total = term if total is None else total + term
        total = total.T
        at = 0
        for count, out in zip(counts, refs[len(flat) + len(quantized) :]):
            out[...] = total[at : at + count * capacity].astype(BF16)
            at += count * capacity

    return pl.pallas_call(
        kernel,
        grid=(width // dt,),
        in_specs=[
            pl.BlockSpec((rows, part), lambda i, block=block: (block, 0))
            for arrays, rows, block in chunks
            for of_part in arrays
            for _ in of_part
        ]
        + [pl.BlockSpec((q.shape[0], dt, part), lambda i: (0, i, 0)) for q in quantized],
        out_specs=[pl.BlockSpec((c * capacity, dt), lambda i: (0, i)) for c in counts],
        out_shape=[pltpu.HBM((c * capacity, width), BF16) for c in counts],
        compiler_params=params(),
        name="back_rows",
    )(*flat, *[in_hbm(q) for q in quantized])


def weight_part(mine, rows_t, chunks, slopes, step_slopes, j, shape, scale, before):
    parts = sum(a.shape[0] for a in slopes)
    _, width, part = slopes[0].shape
    dt = row_tile(width, 896)
    n_chunks = len(chunks)
    flat = [g for arrays, _, _ in chunks for of_part in arrays for g in of_part]
    sizes = [len(of_part) for arrays, _, _ in chunks for of_part in arrays]
    held = 0 if before is None else 1

    def kernel(mine_ref, x_ref, *refs):
        gs = grouped(refs, sizes)
        factors = refs[len(flat) :][: 2 * len(slopes)]
        factors = [r.at[n] for r in factors for n in range(r.shape[0])]
        sl, ts = factors[:parts], factors[parts:]
        out, st = refs[len(flat) + 2 * len(slopes) + held :]
        i = pl.program_id(0)
        for r in range(parts):
            g = jnp.concatenate([total_of(gs[n * parts + r]) for n in range(n_chunks)], axis=0)
            raw = jnp.dot(x_ref[...], g, preferred_element_type=F32)
            column = pl.multiple_of(partner(r, mine_ref[0], parts) * part, part)
            out[0, :, pl.ds(column, part)] = (raw * sl[r][...].astype(F32)).astype(BF16)
            sums = jnp.sum((raw * ts[r][...].astype(F32)).reshape(dt // 8, 8, part), axis=0) * scale
            st[r] = jnp.where(i == 0, sums, st[r] + sums)

    return pl.pallas_call(
        kernel,
        grid_spec=pltpu.PrefetchScalarGridSpec(
            num_scalar_prefetch=1,
            grid=(width // dt,),
            in_specs=[pl.BlockSpec((dt, rows_t.shape[1]), lambda i, m: (i, 0))]
            + [
                pl.BlockSpec((rows, part), lambda i, m, block=block: (block, 0))
                for arrays, rows, block in chunks
                for of_part in arrays
                for _ in of_part
            ]
            + [pl.BlockSpec((a.shape[0], dt, part), lambda i, m: (0, i, 0)) for a in slopes + step_slopes]
            + [pl.BlockSpec(memory_space=pl.ANY)] * held,
            out_specs=[
                pl.BlockSpec((1, dt, parts * part), lambda i, m: (j, i, 0)),
                pl.BlockSpec((parts, 8, part), lambda i, m: (0, 0, 0)),
            ],
        ),
        out_shape=[
            pltpu.HBM(shape, BF16),
            jax.ShapeDtypeStruct((parts, 8, part), F32),
        ],
        input_output_aliases={2 + len(flat) + 2 * len(slopes): 0} if held else {},
        compiler_params=params(),
        name="weight_part",
    )(
        mine,
        in_hbm(rows_t),
        *flat,
        *[in_hbm(a) for a in slopes + step_slopes],
        *(() if before is None else (before,)),
    )


def combine(me, ids_t, returned, groups, local, capacity, earlier_sum=None, final=True):
    _, tok_rows = ids_t.shape
    names = [name for _, _, of_array in returned for name in of_array]
    width = returned[0][0].shape[1]
    dt = row_tile(width, 896)

    held = [] if earlier_sum is None else [earlier_sum]
    dtype = BF16 if final else F32

    def kernel(me_ref, ids_ref, *refs):
        ins, sums, out, pick_ref = refs[: len(returned)], refs[len(returned) : -2], refs[-2], refs[-1]

        @pl.when(pl.program_id(0) == 0)
        def _():
            ids = ids_ref[...]
            member = [named_by(ids, partner(k, me_ref[0], groups) * local + j) for j, k in names]
            pick_ref[...] = picks(jnp.concatenate(member, axis=0), capacity)

        rows = jnp.concatenate([r[...] for r in ins], axis=0)
        total = lax.dot_general(
            pick_ref[...], rows, (((0,), (0,)), ((), ())), preferred_element_type=F32
        )
        for ref in sums:
            total = total + ref[...]
        out[...] = total.astype(dtype)

    return pl.pallas_call(
        kernel,
        grid_spec=pltpu.PrefetchScalarGridSpec(
            num_scalar_prefetch=1,
            grid=(width // dt,),
            in_specs=[pl.BlockSpec(ids_t.shape, lambda i, me: (0, 0))]
            + [
                pl.BlockSpec((len(of_array) * capacity, dt), lambda i, me, block=block: (block, i))
                for _, block, of_array in returned
            ]
            + [pl.BlockSpec((tok_rows, dt), lambda i, me: (0, i)) for _ in held],
            out_specs=pl.BlockSpec((tok_rows, dt), lambda i, me: (0, i)),
            scratch_shapes=[pltpu.VMEM((len(names) * capacity, tok_rows), BF16)],
        ),
        out_shape=jax.ShapeDtypeStruct((tok_rows, width), dtype),
        compiler_params=params(),
        name="combine",
    )(me, ids_t, *[array for array, _, _ in returned], *held)


def per_device(tokens, cotangent, weights, steps, expert_ids):
    groups, parts = lax.axis_size("expert"), lax.axis_size("mp")
    local = weights.shape[0]
    tok_rows, top_k = expert_ids.shape
    capacity = tok_rows // 2
    part = cotangent.shape[2]
    width = tokens.shape[1]
    me, mine = lax.axis_index("expert"), lax.axis_index("mp")
    me_arr = me.astype(jnp.int32)[None]
    mine_arr = mine.astype(jnp.int32)[None]
    expert_swap = lambda x, k: swap(x, "expert", k, groups)
    mp_swap = lambda x, r: swap(x, "mp", r, parts)

    *g_out, own, ids_t, thirds = dispatch(
        me_arr,
        expert_ids.T,
        cotangent.reshape(tok_rows * top_k, part),
        tokens,
        steps,
        groups,
        local,
        capacity,
    )
    near_in = expert_swap(g_out[1], 1)
    g_in = [g_out[0], near_in]
    for k in range(2, groups):
        g_in.append(expert_swap(g_out[k], k))
    of = lambda j, k: g_in[k][j * capacity : (j + 1) * capacity]
    near = [0, 1]
    first = spread(jnp.concatenate([of(j, k) for j in range(local) for k in near] + [thirds], axis=0), parts, False)
    far = {}
    for j in range(local):
        ks = list(range(2, groups))
        if ks:
            rows = jnp.concatenate([of(j, k) for k in ks], axis=0)
            relay = parts == 4 and j == local - 1
            far[j] = [(ks, (spread(rows, parts, relay), rows.shape[0], 0))]
    blocks = [own] + [None] * (groups - 1)
    for k in range(2, groups, 2):
        blocks[k] = expert_swap(own, k)
    for k in range(1, groups, 2):
        blocks[k] = expert_swap(blocks[k - 1], 1)

    pieces = [[] for _ in range(local)]
    at = local * len(near) * capacity
    for j in range(local):
        cuts = [0, 1, parts] if j == 0 else [0, parts // 2, parts]
        for low, high in zip(cuts, cuts[1:]):
            if low < high:
                pieces[j].append(quantize(mine_arr, weights, [a[0] for a in first], at, j, low, high))
    quantized = [[list(a) for a in zip(*of_expert)] for of_expert in pieces]
    rows_t = expert_rows(me_arr, blocks, groups, local, tok_rows, capacity)

    returned, onward, weight_out, partial = [], [], None, []
    scale = QMAX / math.sqrt(width * parts * QMAX)
    for j in range(local):
        values, slopes, step_slopes = quantized[j]
        chunks = [(near, (first, len(near) * capacity, j))] + far.get(j, [])
        ks = [k for of_chunk, _ in chunks for k in of_chunk]
        step = 1 if j == local - 1 else 2
        outs = back_rows([c for _, c in chunks], values, capacity, [step] * (len(ks) // step))
        for k, rows in zip(ks[::step], outs):
            rows = expert_swap(rows, k) if k else in_hbm(rows)
            returned.append((rows, 0, [(j, k)]))
            if step == 2:
                onward.append((rows, j, k + 1))
        weight_out, sums = weight_part(
            mine_arr,
            rows_t[j],
            [c for _, c in chunks],
            slopes,
            step_slopes,
            j,
            weights.shape,
            scale,
            weight_out,
        )
        partial.append(sums)
    for rows, j, k in onward:
        returned.append((expert_swap(rows, 1), 1, [(j, k)]))
    sums = jnp.stack([p.sum(axis=1) for p in partial], axis=1)
    others = [mp_swap(sums[r], r) for r in range(1, parts)]
    step_out = sum(others, sums[0])
    token_out = combine(me_arr, ids_t, returned, groups, local, capacity)
    return (token_out, weight_out, step_out)


def solution(mesh):
    return jax.shard_map(
        per_device,
        mesh=mesh,
        in_specs=(
            P("expert", "mp"),
            P("expert", None, "mp"),
            P("expert", "mp", None),
            P("expert", "mp"),
            P("expert", None),
        ),
        out_specs=(P("expert", "mp"), P("expert", "mp", None), P("expert", "mp")),
        check_vma=False,
    )
```

```python
import math

import jax
import jax.numpy as jnp
from jax import lax
from jax.experimental import pallas as pl
from jax.experimental.pallas import tpu as pltpu
from jax.sharding import PartitionSpec as P


QMAX = 7.0
WIGGLE = 0.9
BF16 = jnp.bfloat16
F32 = jnp.float32

SIN = (3.1415820221481474, -5.167142796288472, 2.5418990269458197, -0.5546361956218614)
SCALED = tuple(math.sqrt(2.0 * WIGGLE) * k for k in SIN)
ROUNDER = 12582912.0


def params(mib=48):
    return pltpu.CompilerParams(vmem_limit_bytes=mib * 1024 * 1024)


def in_hbm(x):
    return pltpu.with_memory_space_constraint(x, pltpu.HBM)


def partner(offset, index, size):
    if size & (size - 1) == 0:
        return index ^ offset
    return (offset - index) % size


def swap(x, axis, offset, size):
    return lax.ppermute(x, axis, [(i, partner(offset, i, size)) for i in range(size)])


def spread(x, parts, relay):
    if not relay:
        return [(x,)] + [(swap(x, "mp", r, parts),) for r in range(1, parts)]
    two = swap(x, "mp", 2, parts)
    one = swap(x, "mp", 1, parts)
    inner = lax.ppermute(x, "mp", [(1, 2), (2, 1)])
    outer = lax.ppermute(two, "mp", [(1, 0), (2, 3)])
    return [(x,), (one,), (two,), (inner, outer)]


def total_of(refs):
    value = refs[0][...]
    for ref in refs[1:]:
        value = value + ref[...]
    return value


def grouped(refs, sizes):
    out, at = [], 0
    for size in sizes:
        out.append(list(refs[at : at + size]))
        at += size
    return out


def row_tile(rows, want):
    tile = min(rows, want)
    while rows % tile:
        tile //= 2
    return tile


def quantize(mine, weights, steps, at, pieces):
    rows_in = -(-3 * weights.shape[0] // 8) * 8
    _, width, full = weights.shape
    part = full // len(steps)
    dt = row_tile(width, 896)
    chunk = row_tile(dt, 16)
    turns = [(j, r) for j, low, high in pieces for r in range(low, high)]
    starts = [sum(high - low for _, low, high in pieces[:n]) for n in range(len(pieces) + 1)]

    def at_turn(g, values):
        out = values[0]
        for n, value in enumerate(values[1:], 1):
            out = jnp.where(g == n, value, out)
        return out

    def kernel(mine_ref, w_ref, *refs):
        step_refs, outs = refs[: len(turns)], refs[len(turns) :]
        thirds = at_turn(pl.program_id(0), [ref[...].astype(F32) for ref in step_refs])

        def piece(j, q_ref, sl_ref, ts_ref):
            step = thirds[3 * j : 3 * j + 1] + thirds[3 * j + 1 : 3 * j + 2] + thirds[3 * j + 2 : 3 * j + 3]
            inv = 1.0 / (QMAX * step)
            step7 = QMAX * step

            def body(i, carry):
                rows = pl.ds(pl.multiple_of(i * chunk, chunk), chunk)
                t = w_ref[0, rows, :].astype(F32) * inv
                u = jnp.tanh(t)
                c = QMAX * u
                r = c - ((c + ROUNDER) - ROUNDER)
                y = r * r
                poly = SCALED[-1]
                for k in SCALED[-2::-1]:
                    poly = poly * y + k
                sine = r * poly
                z = sine * sine
                x = 2.0 * WIGGLE * 1.0000005 - z
                cosine = x * lax.rsqrt(x)
                level = u - (0.5 / (math.pi * QMAX)) * (sine * cosine)
                slopes = (1.0 - WIGGLE + z) * (1.0 - u * u)
                q_ref[0, rows, :] = (step7 * level).astype(BF16)
                sl_ref[0, rows, :] = slopes.astype(BF16)
                ts_ref[0, rows, :] = (level - t * slopes).astype(BF16)
                return carry

            lax.fori_loop(0, dt // chunk, body, 0, unroll=2 if dt // chunk % 2 == 0 else 1)

        for n, (j, _, _) in enumerate(pieces):
            g = pl.program_id(0)
            pl.when((g >= starts[n]) & (g < starts[n + 1]))(
                lambda j=j, n=n: piece(j, *outs[3 * n : 3 * n + 3])
            )

    def weights_map(g, i, mine):
        offset = at_turn(g, [r for _, r in turns])
        return at_turn(g, [j for j, _ in turns]), i, partner(offset, mine[0], len(steps))

    def out_map(n):
        def place(g, i, mine):
            before, after = g < starts[n], g >= starts[n + 1]
            last = starts[n + 1] - starts[n] - 1
            where = jnp.clip(g - starts[n], 0, last)
            return where, jnp.where(before, 0, jnp.where(after, width // dt - 1, i)), 0

        return place

    return pl.pallas_call(
        kernel,
        grid_spec=pltpu.PrefetchScalarGridSpec(
            num_scalar_prefetch=1,
            grid=(len(turns), width // dt),
            in_specs=[pl.BlockSpec((1, dt, part), weights_map)]
            + [pl.BlockSpec((rows_in, part), lambda g, i, mine: (at // rows_in, 0))] * len(turns),
            out_specs=[pl.BlockSpec((1, dt, part), out_map(n)) for n in range(len(pieces)) for _ in range(3)],
        ),
        out_shape=[pltpu.HBM((high - low, width, part), BF16) for _, low, high in pieces for _ in range(3)],
        compiler_params=params(),
        name="quantize",
    )(mine, weights, *[steps[r] for _, r in turns])


def picks(member, capacity):
    n, tok_rows = member.shape
    before = jnp.dot(member.astype(BF16), earlier(tok_rows), preferred_element_type=F32)
    code = jnp.where(member > 0.5, before, -1.0).astype(jnp.int32)
    slot = lax.broadcasted_iota(jnp.int32, (capacity, tok_rows), 0)
    rows = [(slot == code[i : i + 1]).astype(F32) for i in range(n)]
    return jnp.concatenate(rows, axis=0).astype(BF16)


def named_by(ids, e):
    return jnp.sum((ids == e.astype(F32)).astype(F32), axis=0, keepdims=True)


def earlier(n):
    rows = lax.broadcasted_iota(jnp.int32, (n, n), 0)
    return (rows < lax.broadcasted_iota(jnp.int32, (n, n), 1)).astype(F32).astype(BF16)


def dispatch(me, ids, cot, tokens, steps, groups, local, capacity):
    routes, part = cot.shape
    top_k, tok_rows = ids.shape
    width = tokens.shape[1]
    experts = groups * local
    step_rows = -(-3 * local // 8) * 8

    def kernel(me_ref, ids_hbm, steps_hbm, cot_hbm, tok_hbm, *refs):
        outs, own_ref, ids_out, steps_out = refs[:groups], *refs[groups : groups + 3]
        code_ref, ids_ref, steps_ref, cot_ref, sems = refs[groups + 3 :]
        ids_copy = pltpu.make_async_copy(ids_hbm, ids_ref, sems.at[2])
        steps_copy = pltpu.make_async_copy(steps_hbm, steps_ref, sems.at[3])
        ids_copy.start()
        steps_copy.start()
        cot_copy = pltpu.make_async_copy(cot_hbm, cot_ref, sems.at[0])
        tok_copy = pltpu.make_async_copy(tok_hbm, own_ref.at[:tok_rows, :], sems.at[1])
        cot_copy.start()
        tok_copy.start()
        ids_copy.wait()
        steps_copy.wait()
        step = steps_ref[...]
        high = step.astype(BF16).astype(F32)
        middle = (step - high).astype(BF16).astype(F32)
        low = step - high - middle
        thirds = [x[j : j + 1] for j in range(local) for x in (high, middle, low)]
        thirds += [jnp.zeros_like(thirds[0])] * (step_rows - 3 * local)
        steps_out[...] = jnp.concatenate(thirds, axis=0).astype(BF16)
        ids_t = ids_ref[...].astype(F32)
        ids_out[...] = ids_t
        own_ref[tok_rows:, :] = jnp.zeros((top_k, width), BF16)
        own_ref[tok_rows:, :tok_rows] = ids_t.astype(BF16)
        route = lax.broadcasted_iota(jnp.int32, (tok_rows, routes), 1)
        token = lax.broadcasted_iota(jnp.int32, (tok_rows, routes), 0)
        spread = jnp.dot(
            ids_t,
            (route // top_k == token).astype(F32),
            precision=lax.Precision.HIGHEST,
            preferred_element_type=F32,
        )
        choice = lax.broadcasted_iota(jnp.int32, (top_k, routes), 1) % top_k
        mask = choice == lax.broadcasted_iota(jnp.int32, (top_k, routes), 0)
        ids_row = jnp.sum(jnp.where(mask, spread, 0.0), axis=0, keepdims=True)
        ids_row = jnp.round(ids_row).astype(jnp.int32)
        expert = lax.broadcasted_iota(jnp.int32, (experts, routes), 0)
        named = expert == ids_row
        before = jnp.dot(named.astype(F32).astype(BF16), earlier(routes), preferred_element_type=F32)
        code_ref[...] = jnp.where(named, before.astype(jnp.int32), -1)
        slot = lax.broadcasted_iota(jnp.int32, (capacity, routes), 0)
        cot_copy.wait()
        size = local * capacity
        for low in range(0, groups, 4):
            ks = range(low, min(low + 4, groups))
            codes = [
                code_ref[pl.ds(partner(k, me_ref[0], groups) * local + j, 1), :]
                for k in ks
                for j in range(local)
            ]
            pick = jnp.concatenate([(slot == code).astype(F32) for code in codes], axis=0)
            rows = jnp.dot(pick.astype(BF16), cot_ref[...], preferred_element_type=F32).astype(BF16)
            for n, k in enumerate(ks):
                outs[k][...] = rows[n * size : (n + 1) * size]
        tok_copy.wait()

    whole = lambda shape: pl.BlockSpec(shape, lambda i, me: (0, 0))
    return pl.pallas_call(
        kernel,
        grid_spec=pltpu.PrefetchScalarGridSpec(
            num_scalar_prefetch=1,
            grid=(1,),
            in_specs=[pl.BlockSpec(memory_space=pltpu.HBM)] * 4,
            out_specs=[whole((local * capacity, part))] * groups
            + [whole((tok_rows + top_k, width)), whole((top_k, tok_rows)), whole((step_rows, part))],
            scratch_shapes=[
                pltpu.VMEM((experts, routes), jnp.int32),
                pltpu.VMEM(ids.shape, jnp.int32),
                pltpu.VMEM(steps.shape, F32),
                pltpu.VMEM(cot.shape, BF16),
                pltpu.SemaphoreType.DMA((4,)),
            ],
        ),
        out_shape=[jax.ShapeDtypeStruct((local * capacity, part), BF16)] * groups
        + [
            jax.ShapeDtypeStruct((tok_rows + top_k, width), BF16),
            jax.ShapeDtypeStruct((top_k, tok_rows), F32),
            jax.ShapeDtypeStruct((step_rows, part), BF16),
        ],
        compiler_params=params(),
        name="dispatch",
    )(
        me,
        *[in_hbm(x) for x in (ids, steps, cot, tokens)],
    )


def expert_rows(me, blocks, groups, local, tok_rows, capacity):
    width = blocks[0].shape[1]
    dt = row_tile(width, 896)

    def kernel(me_ref, *refs):
        ids_refs, ins = refs[:groups], refs[groups : 2 * groups]
        outs, pick_ref = refs[2 * groups : -1], refs[-1]

        @pl.when(pl.program_id(0) == 0)
        def _():
            ids = [ids_refs[k][tok_rows:, :tok_rows].astype(F32) for k in range(groups)]
            member = [named_by(i, me_ref[0] * local + j) for i in ids for j in range(local)]
            pick_ref[...] = picks(jnp.concatenate(member, axis=0), capacity)

        size = local * capacity
        rows = [
            jnp.dot(
                pick_ref[k * size : (k + 1) * size, :],
                ins[k][:tok_rows, :],
                preferred_element_type=F32,
            )
            for k in range(groups)
        ]
        for j in range(local):
            of_expert = [r[j * capacity : (j + 1) * capacity] for r in rows]
            outs[j][...] = jnp.concatenate(of_expert, axis=0).T.astype(BF16)

    rows_in = blocks[0].shape[0]
    return pl.pallas_call(
        kernel,
        grid_spec=pltpu.PrefetchScalarGridSpec(
            num_scalar_prefetch=1,
            grid=(width // dt,),
            in_specs=[pl.BlockSpec((rows_in, dt), lambda i, me: (0, 0))] * groups
            + [pl.BlockSpec((rows_in, dt), lambda i, me: (0, i))] * groups,
            out_specs=[pl.BlockSpec((dt, groups * capacity), lambda i, me: (i, 0))] * local,
            scratch_shapes=[pltpu.VMEM((local * groups * capacity, tok_rows), BF16)],
        ),
        out_shape=[pltpu.HBM((width, groups * capacity), BF16)] * local,
        compiler_params=params(),
        name="expert_rows",
    )(me, *blocks, *blocks)


def back_rows(chunks, quantized, capacity, counts):
    parts = sum(q.shape[0] for q in quantized)
    _, width, part = quantized[0].shape
    dt = row_tile(width, 896)
    flat = [g for arrays, _, _ in chunks for of_part in arrays for g in of_part]
    sizes = [len(of_part) for arrays, _, _ in chunks for of_part in arrays]

    def kernel(*refs):
        q_refs = [r.at[n] for r in refs[len(flat) :][: len(quantized)] for n in range(r.shape[0])]
        gs = grouped(refs, sizes)
        total = None
        for r in range(parts):
            rows = jnp.concatenate([total_of(gs[n * parts + r]) for n in range(len(chunks))], axis=0)
            term = lax.dot_general(
                q_refs[r][...], rows, (((1,), (1,)), ((), ())), preferred_element_type=F32
            )
            total = term if total is None else total + term
        total = total.T
        at = 0
        for count, out in zip(counts, refs[len(flat) + len(quantized) :]):
            out[...] = total[at : at + count * capacity].astype(BF16)
            at += count * capacity

    return pl.pallas_call(
        kernel,
        grid=(width // dt,),
        in_specs=[
            pl.BlockSpec((rows, part), lambda i, block=block: (block, 0))
            for arrays, rows, block in chunks
            for of_part in arrays
            for _ in of_part
        ]
        + [pl.BlockSpec((q.shape[0], dt, part), lambda i: (0, i, 0)) for q in quantized],
        out_specs=[pl.BlockSpec((c * capacity, dt), lambda i: (0, i)) for c in counts],
        out_shape=[pltpu.HBM((c * capacity, width), BF16) for c in counts],
        compiler_params=params(),
        name="back_rows",
    )(*flat, *[in_hbm(q) for q in quantized])


def weight_part(mine, rows_t, chunks, slopes, step_slopes, j, shape, scale, before):
    parts = sum(a.shape[0] for a in slopes)
    _, width, part = slopes[0].shape
    dt = row_tile(width, 896)
    n_chunks = len(chunks)
    flat = [g for arrays, _, _ in chunks for of_part in arrays for g in of_part]
    sizes = [len(of_part) for arrays, _, _ in chunks for of_part in arrays]
    held = 0 if before is None else 1

    def kernel(mine_ref, x_ref, *refs):
        gs = grouped(refs, sizes)
        factors = refs[len(flat) :][: 2 * len(slopes)]
        factors = [r.at[n] for r in factors for n in range(r.shape[0])]
        sl, ts = factors[:parts], factors[parts:]
        out, st = refs[len(flat) + 2 * len(slopes) + held :]
        i = pl.program_id(0)
        for r in range(parts):
            g = jnp.concatenate([total_of(gs[n * parts + r]) for n in range(n_chunks)], axis=0)
            raw = jnp.dot(x_ref[...], g, preferred_element_type=F32)
            column = pl.multiple_of(partner(r, mine_ref[0], parts) * part, part)
            out[0, :, pl.ds(column, part)] = (raw * sl[r][...].astype(F32)).astype(BF16)
            sums = jnp.sum((raw * ts[r][...].astype(F32)).reshape(dt // 8, 8, part), axis=0) * scale
            st[r] = jnp.where(i == 0, sums, st[r] + sums)

    return pl.pallas_call(
        kernel,
        grid_spec=pltpu.PrefetchScalarGridSpec(
            num_scalar_prefetch=1,
            grid=(width // dt,),
            in_specs=[pl.BlockSpec((dt, rows_t.shape[1]), lambda i, m: (i, 0))]
            + [
                pl.BlockSpec((rows, part), lambda i, m, block=block: (block, 0))
                for arrays, rows, block in chunks
                for of_part in arrays
                for _ in of_part
            ]
            + [pl.BlockSpec((a.shape[0], dt, part), lambda i, m: (0, i, 0)) for a in slopes + step_slopes]
            + [pl.BlockSpec(memory_space=pl.ANY)] * held,
            out_specs=[
                pl.BlockSpec((1, dt, parts * part), lambda i, m: (j, i, 0)),
                pl.BlockSpec((parts, 8, part), lambda i, m: (0, 0, 0)),
            ],
        ),
        out_shape=[
            pltpu.HBM(shape, BF16),
            jax.ShapeDtypeStruct((parts, 8, part), F32),
        ],
        input_output_aliases={2 + len(flat) + 2 * len(slopes): 0} if held else {},
        compiler_params=params(),
        name="weight_part",
    )(
        mine,
        in_hbm(rows_t),
        *flat,
        *[in_hbm(a) for a in slopes + step_slopes],
        *(() if before is None else (before,)),
    )


def combine(me, ids_t, returned, groups, local, capacity, earlier_sum=None, final=True):
    _, tok_rows = ids_t.shape
    names = [name for _, _, of_array in returned for name in of_array]
    width = returned[0][0].shape[1]
    dt = row_tile(width, 896)

    held = [] if earlier_sum is None else [earlier_sum]
    dtype = BF16 if final else F32

    def kernel(me_ref, ids_ref, *refs):
        ins, sums, out, pick_ref = refs[: len(returned)], refs[len(returned) : -2], refs[-2], refs[-1]

        @pl.when(pl.program_id(0) == 0)
        def _():
            ids = ids_ref[...]
            member = [named_by(ids, partner(k, me_ref[0], groups) * local + j) for j, k in names]
            pick_ref[...] = picks(jnp.concatenate(member, axis=0), capacity)

        rows = jnp.concatenate([r[...] for r in ins], axis=0)
        total = lax.dot_general(
            pick_ref[...], rows, (((0,), (0,)), ((), ())), preferred_element_type=F32
        )
        for ref in sums:
            total = total + ref[...]
        out[...] = total.astype(dtype)

    return pl.pallas_call(
        kernel,
        grid_spec=pltpu.PrefetchScalarGridSpec(
            num_scalar_prefetch=1,
            grid=(width // dt,),
            in_specs=[pl.BlockSpec(ids_t.shape, lambda i, me: (0, 0))]
            + [
                pl.BlockSpec((len(of_array) * capacity, dt), lambda i, me, block=block: (block, i))
                for _, block, of_array in returned
            ]
            + [pl.BlockSpec((tok_rows, dt), lambda i, me: (0, i)) for _ in held],
            out_specs=pl.BlockSpec((tok_rows, dt), lambda i, me: (0, i)),
            scratch_shapes=[pltpu.VMEM((len(names) * capacity, tok_rows), BF16)],
        ),
        out_shape=jax.ShapeDtypeStruct((tok_rows, width), dtype),
        compiler_params=params(),
        name="combine",
    )(me, ids_t, *[array for array, _, _ in returned], *held)


def per_device(tokens, cotangent, weights, steps, expert_ids):
    groups, parts = lax.axis_size("expert"), lax.axis_size("mp")
    local = weights.shape[0]
    tok_rows, top_k = expert_ids.shape
    capacity = tok_rows // 2
    part = cotangent.shape[2]
    width = tokens.shape[1]
    me, mine = lax.axis_index("expert"), lax.axis_index("mp")
    me_arr = me.astype(jnp.int32)[None]
    mine_arr = mine.astype(jnp.int32)[None]
    expert_swap = lambda x, k: swap(x, "expert", k, groups)
    mp_swap = lambda x, r: swap(x, "mp", r, parts)

    *g_out, own, ids_t, thirds = dispatch(
        me_arr,
        expert_ids.T,
        cotangent.reshape(tok_rows * top_k, part),
        tokens,
        steps,
        groups,
        local,
        capacity,
    )
    near_in = expert_swap(g_out[1], 1)
    g_in = [g_out[0], near_in]
    for k in range(2, groups):
        g_in.append(expert_swap(g_out[k], k))
    of = lambda j, k: g_in[k][j * capacity : (j + 1) * capacity]
    near = [0, 1]
    first = spread(jnp.concatenate([of(j, k) for j in range(local) for k in near] + [thirds], axis=0), parts, False)
    far = {}
    for j in range(local):
        ks = list(range(2, groups))
        if ks:
            rows = jnp.concatenate([of(j, k) for k in ks], axis=0)
            relay = parts == 4 and j == local - 1
            far[j] = [(ks, (spread(rows, parts, relay), rows.shape[0], 0))]
    blocks = [own] + [None] * (groups - 1)
    for k in range(2, groups, 2):
        blocks[k] = expert_swap(own, k)
    for k in range(1, groups, 2):
        blocks[k] = expert_swap(blocks[k - 1], 1)

    pieces = [[] for _ in range(local)]
    at = local * len(near) * capacity
    half = max(parts // 2, 1)
    later = range(1, local)
    calls = [
        [(j, 0, 1) for j in range(local)],
        [(j, 1, half) for j in later if half > 1] + [(0, 1, parts)] * (parts > 1),
        [(j, half, parts) for j in later if half < parts],
    ]
    for call in calls:
        if call:
            outs = quantize(mine_arr, weights, [a[0] for a in first], at, call)
            for m, (j, _, _) in enumerate(call):
                pieces[j].append(outs[3 * m : 3 * m + 3])
    quantized = [[list(a) for a in zip(*of_expert)] for of_expert in pieces]
    rows_t = expert_rows(me_arr, blocks, groups, local, tok_rows, capacity)

    returned, onward, weight_out, partial = [], [], None, []
    scale = QMAX / math.sqrt(width * parts * QMAX)
    for j in range(local):
        values, slopes, step_slopes = quantized[j]
        chunks = [(near, (first, len(near) * capacity, j))] + far.get(j, [])
        ks = [k for of_chunk, _ in chunks for k in of_chunk]
        step = 1 if j == local - 1 else 2
        outs = back_rows([c for _, c in chunks], values, capacity, [step] * (len(ks) // step))
        for k, rows in zip(ks[::step], outs):
            rows = expert_swap(rows, k) if k else in_hbm(rows)
            returned.append((rows, 0, [(j, k)]))
            if step == 2:
                onward.append((rows, j, k + 1))
        weight_out, sums = weight_part(
            mine_arr,
            rows_t[j],
            [c for _, c in chunks],
            slopes,
            step_slopes,
            j,
            weights.shape,
            scale,
            weight_out,
        )
        partial.append(sums)
    for rows, j, k in onward:
        returned.append((expert_swap(rows, 1), 1, [(j, k)]))
    sums = jnp.stack([p.sum(axis=1) for p in partial], axis=1)
    others = [mp_swap(sums[r], r) for r in range(1, parts)]
    step_out = sum(others, sums[0])
    token_out = combine(me_arr, ids_t, returned, groups, local, capacity)
    return (token_out, weight_out, step_out)


def solution(mesh):
    return jax.shard_map(
        per_device,
        mesh=mesh,
        in_specs=(
            P("expert", "mp"),
            P("expert", None, "mp"),
            P("expert", "mp", None),
            P("expert", "mp"),
            P("expert", None),
        ),
        out_specs=(P("expert", "mp"), P("expert", "mp", None), P("expert", "mp")),
        check_vma=False,
    )
```

```python
import math

import jax
import jax.numpy as jnp
from jax import lax
from jax.experimental import pallas as pl
from jax.experimental.pallas import tpu as pltpu
from jax.sharding import PartitionSpec as P


QMAX = 7.0
WIGGLE = 0.9
BF16 = jnp.bfloat16
F32 = jnp.float32

SIN = (3.1415820221481474, -5.167142796288472, 2.5418990269458197, -0.5546361956218614)
SCALED = tuple(math.sqrt(2.0 * WIGGLE) * k for k in SIN)
ROUNDER = 12582912.0


def params(mib=48):
    return pltpu.CompilerParams(vmem_limit_bytes=mib * 1024 * 1024)


def in_hbm(x):
    return pltpu.with_memory_space_constraint(x, pltpu.HBM)


def partner(offset, index, size):
    if size & (size - 1) == 0:
        return index ^ offset
    return (offset - index) % size


def swap(x, axis, offset, size):
    return lax.ppermute(x, axis, [(i, partner(offset, i, size)) for i in range(size)])


def spread(x, parts, relay):
    if not relay:
        return [(x,)] + [(swap(x, "mp", r, parts),) for r in range(1, parts)]
    two = swap(x, "mp", 2, parts)
    one = swap(x, "mp", 1, parts)
    inner = lax.ppermute(x, "mp", [(1, 2), (2, 1)])
    outer = lax.ppermute(two, "mp", [(1, 0), (2, 3)])
    return [(x,), (one,), (two,), (inner, outer)]


def total_of(refs):
    value = refs[0][...]
    for ref in refs[1:]:
        value = value + ref[...]
    return value


def grouped(refs, sizes):
    out, at = [], 0
    for size in sizes:
        out.append(list(refs[at : at + size]))
        at += size
    return out


def row_tile(rows, want):
    tile = min(rows, want)
    while rows % tile:
        tile //= 2
    return tile


def quantize(mine, weights, steps, at, pieces):
    rows_in = -(-3 * weights.shape[0] // 8) * 8
    _, width, full = weights.shape
    part = full // len(steps)
    dt = row_tile(width, 896)
    chunk = row_tile(dt, 16)
    turns = [(j, r) for j, low, high in pieces for r in range(low, high)]
    starts = [sum(high - low for _, low, high in pieces[:n]) for n in range(len(pieces) + 1)]

    def at_turn(g, values):
        out = values[0]
        for n, value in enumerate(values[1:], 1):
            out = jnp.where(g == n, value, out)
        return out

    def kernel(mine_ref, w_ref, *refs):
        step_refs, outs = refs[: len(turns)], refs[len(turns) :]
        thirds = at_turn(pl.program_id(0), [ref[...].astype(F32) for ref in step_refs])

        def piece(j, q_ref, sl_ref, ts_ref):
            step = thirds[3 * j : 3 * j + 1] + thirds[3 * j + 1 : 3 * j + 2] + thirds[3 * j + 2 : 3 * j + 3]
            inv = 1.0 / (QMAX * step)
            step7 = QMAX * step

            def body(i, carry):
                rows = pl.ds(pl.multiple_of(i * chunk, chunk), chunk)
                t = w_ref[0, rows, :].astype(F32) * inv
                u = jnp.tanh(t)
                c = QMAX * u
                r = c - ((c + ROUNDER) - ROUNDER)
                y = r * r
                poly = SCALED[-1]
                for k in SCALED[-2::-1]:
                    poly = poly * y + k
                sine = r * poly
                z = sine * sine
                x = 2.0 * WIGGLE * 1.0000005 - z
                cosine = x * lax.rsqrt(x)
                level = u - (0.5 / (math.pi * QMAX)) * (sine * cosine)
                slopes = (1.0 - WIGGLE + z) * (1.0 - u * u)
                q_ref[0, rows, :] = (step7 * level).astype(BF16)
                sl_ref[0, rows, :] = slopes.astype(BF16)
                ts_ref[0, rows, :] = (level - t * slopes).astype(BF16)
                return carry

            lax.fori_loop(0, dt // chunk, body, 0, unroll=4 if dt // chunk % 4 == 0 else 1)

        for n, (j, _, _) in enumerate(pieces):
            g = pl.program_id(0)
            pl.when((g >= starts[n]) & (g < starts[n + 1]))(
                lambda j=j, n=n: piece(j, *outs[3 * n : 3 * n + 3])
            )

    def weights_map(g, i, mine):
        offset = at_turn(g, [r for _, r in turns])
        return at_turn(g, [j for j, _ in turns]), i, partner(offset, mine[0], len(steps))

    def out_map(n):
        def place(g, i, mine):
            before, after = g < starts[n], g >= starts[n + 1]
            last = starts[n + 1] - starts[n] - 1
            where = jnp.clip(g - starts[n], 0, last)
            return where, jnp.where(before, 0, jnp.where(after, width // dt - 1, i)), 0

        return place

    return pl.pallas_call(
        kernel,
        grid_spec=pltpu.PrefetchScalarGridSpec(
            num_scalar_prefetch=1,
            grid=(len(turns), width // dt),
            in_specs=[pl.BlockSpec((1, dt, part), weights_map)]
            + [pl.BlockSpec((rows_in, part), lambda g, i, mine: (at // rows_in, 0))] * len(turns),
            out_specs=[pl.BlockSpec((1, dt, part), out_map(n)) for n in range(len(pieces)) for _ in range(3)],
        ),
        out_shape=[pltpu.HBM((high - low, width, part), BF16) for _, low, high in pieces for _ in range(3)],
        compiler_params=params(),
        name="quantize",
    )(mine, weights, *[steps[r] for _, r in turns])


def picks(member, capacity):
    n, tok_rows = member.shape
    before = jnp.dot(member.astype(BF16), earlier(tok_rows), preferred_element_type=F32)
    code = jnp.where(member > 0.5, before, -1.0).astype(jnp.int32)
    slot = lax.broadcasted_iota(jnp.int32, (capacity, tok_rows), 0)
    rows = [(slot == code[i : i + 1]).astype(F32) for i in range(n)]
    return jnp.concatenate(rows, axis=0).astype(BF16)


def named_by(ids, e):
    return jnp.sum((ids == e.astype(F32)).astype(F32), axis=0, keepdims=True)


def earlier(n):
    rows = lax.broadcasted_iota(jnp.int32, (n, n), 0)
    return (rows < lax.broadcasted_iota(jnp.int32, (n, n), 1)).astype(F32).astype(BF16)


def dispatch(me, ids, cot, tokens, steps, groups, local, capacity):
    routes, part = cot.shape
    top_k, tok_rows = ids.shape
    width = tokens.shape[1]
    experts = groups * local
    step_rows = -(-3 * local // 8) * 8

    def kernel(me_ref, ids_hbm, steps_hbm, cot_hbm, tok_hbm, *refs):
        outs, own_ref, ids_out, steps_out = refs[:groups], *refs[groups : groups + 3]
        code_ref, ids_ref, steps_ref, cot_ref, sems = refs[groups + 3 :]
        ids_copy = pltpu.make_async_copy(ids_hbm, ids_ref, sems.at[2])
        steps_copy = pltpu.make_async_copy(steps_hbm, steps_ref, sems.at[3])
        ids_copy.start()
        steps_copy.start()
        cot_copy = pltpu.make_async_copy(cot_hbm, cot_ref, sems.at[0])
        tok_copy = pltpu.make_async_copy(tok_hbm, own_ref.at[:tok_rows, :], sems.at[1])
        cot_copy.start()
        tok_copy.start()
        ids_copy.wait()
        steps_copy.wait()
        step = steps_ref[...]
        high = step.astype(BF16).astype(F32)
        middle = (step - high).astype(BF16).astype(F32)
        low = step - high - middle
        thirds = [x[j : j + 1] for j in range(local) for x in (high, middle, low)]
        thirds += [jnp.zeros_like(thirds[0])] * (step_rows - 3 * local)
        steps_out[...] = jnp.concatenate(thirds, axis=0).astype(BF16)
        ids_t = ids_ref[...].astype(F32)
        ids_out[...] = ids_t
        own_ref[tok_rows:, :] = jnp.zeros((top_k, width), BF16)
        own_ref[tok_rows:, :tok_rows] = ids_t.astype(BF16)
        route = lax.broadcasted_iota(jnp.int32, (tok_rows, routes), 1)
        token = lax.broadcasted_iota(jnp.int32, (tok_rows, routes), 0)
        spread = jnp.dot(
            ids_t,
            (route // top_k == token).astype(F32),
            precision=lax.Precision.HIGHEST,
            preferred_element_type=F32,
        )
        choice = lax.broadcasted_iota(jnp.int32, (top_k, routes), 1) % top_k
        mask = choice == lax.broadcasted_iota(jnp.int32, (top_k, routes), 0)
        ids_row = jnp.sum(jnp.where(mask, spread, 0.0), axis=0, keepdims=True)
        ids_row = jnp.round(ids_row).astype(jnp.int32)
        expert = lax.broadcasted_iota(jnp.int32, (experts, routes), 0)
        named = expert == ids_row
        before = jnp.dot(named.astype(F32).astype(BF16), earlier(routes), preferred_element_type=F32)
        code_ref[...] = jnp.where(named, before.astype(jnp.int32), -1)
        slot = lax.broadcasted_iota(jnp.int32, (capacity, routes), 0)
        cot_copy.wait()
        size = local * capacity
        for low in range(0, groups, 4):
            ks = range(low, min(low + 4, groups))
            codes = [
                code_ref[pl.ds(partner(k, me_ref[0], groups) * local + j, 1), :]
                for k in ks
                for j in range(local)
            ]
            pick = jnp.concatenate([(slot == code).astype(F32) for code in codes], axis=0)
            rows = jnp.dot(pick.astype(BF16), cot_ref[...], preferred_element_type=F32).astype(BF16)
            for n, k in enumerate(ks):
                outs[k][...] = rows[n * size : (n + 1) * size]
        tok_copy.wait()

    whole = lambda shape: pl.BlockSpec(shape, lambda i, me: (0, 0))
    return pl.pallas_call(
        kernel,
        grid_spec=pltpu.PrefetchScalarGridSpec(
            num_scalar_prefetch=1,
            grid=(1,),
            in_specs=[pl.BlockSpec(memory_space=pltpu.HBM)] * 4,
            out_specs=[whole((local * capacity, part))] * groups
            + [whole((tok_rows + top_k, width)), whole((top_k, tok_rows)), whole((step_rows, part))],
            scratch_shapes=[
                pltpu.VMEM((experts, routes), jnp.int32),
                pltpu.VMEM(ids.shape, jnp.int32),
                pltpu.VMEM(steps.shape, F32),
                pltpu.VMEM(cot.shape, BF16),
                pltpu.SemaphoreType.DMA((4,)),
            ],
        ),
        out_shape=[jax.ShapeDtypeStruct((local * capacity, part), BF16)] * groups
        + [
            jax.ShapeDtypeStruct((tok_rows + top_k, width), BF16),
            jax.ShapeDtypeStruct((top_k, tok_rows), F32),
            jax.ShapeDtypeStruct((step_rows, part), BF16),
        ],
        compiler_params=params(),
        name="dispatch",
    )(
        me,
        *[in_hbm(x) for x in (ids, steps, cot, tokens)],
    )


def expert_rows(me, blocks, groups, local, tok_rows, capacity):
    width = blocks[0].shape[1]
    dt = row_tile(width, 896)

    def kernel(me_ref, *refs):
        ids_refs, ins = refs[:groups], refs[groups : 2 * groups]
        outs, pick_ref = refs[2 * groups : -1], refs[-1]

        @pl.when(pl.program_id(0) == 0)
        def _():
            ids = [ids_refs[k][tok_rows:, :tok_rows].astype(F32) for k in range(groups)]
            member = [named_by(i, me_ref[0] * local + j) for i in ids for j in range(local)]
            pick_ref[...] = picks(jnp.concatenate(member, axis=0), capacity)

        size = local * capacity
        rows = [
            jnp.dot(
                pick_ref[k * size : (k + 1) * size, :],
                ins[k][:tok_rows, :],
                preferred_element_type=F32,
            )
            for k in range(groups)
        ]
        for j in range(local):
            of_expert = [r[j * capacity : (j + 1) * capacity] for r in rows]
            outs[j][...] = jnp.concatenate(of_expert, axis=0).T.astype(BF16)

    rows_in = blocks[0].shape[0]
    return pl.pallas_call(
        kernel,
        grid_spec=pltpu.PrefetchScalarGridSpec(
            num_scalar_prefetch=1,
            grid=(width // dt,),
            in_specs=[pl.BlockSpec((rows_in, dt), lambda i, me: (0, 0))] * groups
            + [pl.BlockSpec((rows_in, dt), lambda i, me: (0, i))] * groups,
            out_specs=[pl.BlockSpec((dt, groups * capacity), lambda i, me: (i, 0))] * local,
            scratch_shapes=[pltpu.VMEM((local * groups * capacity, tok_rows), BF16)],
        ),
        out_shape=[pltpu.HBM((width, groups * capacity), BF16)] * local,
        compiler_params=params(),
        name="expert_rows",
    )(me, *blocks, *blocks)


def back_rows(chunks, quantized, capacity, counts):
    parts = sum(q.shape[0] for q in quantized)
    _, width, part = quantized[0].shape
    dt = row_tile(width, 896)
    flat = [g for arrays, _, _ in chunks for of_part in arrays for g in of_part]
    sizes = [len(of_part) for arrays, _, _ in chunks for of_part in arrays]

    def kernel(*refs):
        q_refs = [r.at[n] for r in refs[len(flat) :][: len(quantized)] for n in range(r.shape[0])]
        gs = grouped(refs, sizes)
        total = None
        for r in range(parts):
            rows = jnp.concatenate([total_of(gs[n * parts + r]) for n in range(len(chunks))], axis=0)
            term = lax.dot_general(
                q_refs[r][...], rows, (((1,), (1,)), ((), ())), preferred_element_type=F32
            )
            total = term if total is None else total + term
        total = total.T
        at = 0
        for count, out in zip(counts, refs[len(flat) + len(quantized) :]):
            out[...] = total[at : at + count * capacity].astype(BF16)
            at += count * capacity

    return pl.pallas_call(
        kernel,
        grid=(width // dt,),
        in_specs=[
            pl.BlockSpec((rows, part), lambda i, block=block: (block, 0))
            for arrays, rows, block in chunks
            for of_part in arrays
            for _ in of_part
        ]
        + [pl.BlockSpec((q.shape[0], dt, part), lambda i: (0, i, 0)) for q in quantized],
        out_specs=[pl.BlockSpec((c * capacity, dt), lambda i: (0, i)) for c in counts],
        out_shape=[pltpu.HBM((c * capacity, width), BF16) for c in counts],
        compiler_params=params(),
        name="back_rows",
    )(*flat, *[in_hbm(q) for q in quantized])


def weight_part(mine, rows_t, chunks, slopes, step_slopes, j, shape, scale, before):
    parts = sum(a.shape[0] for a in slopes)
    _, width, part = slopes[0].shape
    dt = row_tile(width, 896)
    n_chunks = len(chunks)
    flat = [g for arrays, _, _ in chunks for of_part in arrays for g in of_part]
    sizes = [len(of_part) for arrays, _, _ in chunks for of_part in arrays]
    held = 0 if before is None else 1

    def kernel(mine_ref, x_ref, *refs):
        gs = grouped(refs, sizes)
        factors = refs[len(flat) :][: 2 * len(slopes)]
        factors = [r.at[n] for r in factors for n in range(r.shape[0])]
        sl, ts = factors[:parts], factors[parts:]
        out, st = refs[len(flat) + 2 * len(slopes) + held :]
        i = pl.program_id(0)
        for r in range(parts):
            g = jnp.concatenate([total_of(gs[n * parts + r]) for n in range(n_chunks)], axis=0)
            raw = jnp.dot(x_ref[...], g, preferred_element_type=F32)
            column = pl.multiple_of(partner(r, mine_ref[0], parts) * part, part)
            out[0, :, pl.ds(column, part)] = (raw * sl[r][...].astype(F32)).astype(BF16)
            sums = jnp.sum((raw * ts[r][...].astype(F32)).reshape(dt // 8, 8, part), axis=0) * scale
            st[r] = jnp.where(i == 0, sums, st[r] + sums)

    return pl.pallas_call(
        kernel,
        grid_spec=pltpu.PrefetchScalarGridSpec(
            num_scalar_prefetch=1,
            grid=(width // dt,),
            in_specs=[pl.BlockSpec((dt, rows_t.shape[1]), lambda i, m: (i, 0))]
            + [
                pl.BlockSpec((rows, part), lambda i, m, block=block: (block, 0))
                for arrays, rows, block in chunks
                for of_part in arrays
                for _ in of_part
            ]
            + [pl.BlockSpec((a.shape[0], dt, part), lambda i, m: (0, i, 0)) for a in slopes + step_slopes]
            + [pl.BlockSpec(memory_space=pl.ANY)] * held,
            out_specs=[
                pl.BlockSpec((1, dt, parts * part), lambda i, m: (j, i, 0)),
                pl.BlockSpec((parts, 8, part), lambda i, m: (0, 0, 0)),
            ],
        ),
        out_shape=[
            pltpu.HBM(shape, BF16),
            jax.ShapeDtypeStruct((parts, 8, part), F32),
        ],
        input_output_aliases={2 + len(flat) + 2 * len(slopes): 0} if held else {},
        compiler_params=params(),
        name="weight_part",
    )(
        mine,
        in_hbm(rows_t),
        *flat,
        *[in_hbm(a) for a in slopes + step_slopes],
        *(() if before is None else (before,)),
    )


def combine(me, ids_t, returned, groups, local, capacity, earlier_sum=None, final=True):
    _, tok_rows = ids_t.shape
    names = [name for _, _, of_array in returned for name in of_array]
    width = returned[0][0].shape[1]
    dt = row_tile(width, 896)

    held = [] if earlier_sum is None else [earlier_sum]
    dtype = BF16 if final else F32

    def kernel(me_ref, ids_ref, *refs):
        ins, sums, out, pick_ref = refs[: len(returned)], refs[len(returned) : -2], refs[-2], refs[-1]

        @pl.when(pl.program_id(0) == 0)
        def _():
            ids = ids_ref[...]
            member = [named_by(ids, partner(k, me_ref[0], groups) * local + j) for j, k in names]
            pick_ref[...] = picks(jnp.concatenate(member, axis=0), capacity)

        rows = jnp.concatenate([r[...] for r in ins], axis=0)
        total = lax.dot_general(
            pick_ref[...], rows, (((0,), (0,)), ((), ())), preferred_element_type=F32
        )
        for ref in sums:
            total = total + ref[...]
        out[...] = total.astype(dtype)

    return pl.pallas_call(
        kernel,
        grid_spec=pltpu.PrefetchScalarGridSpec(
            num_scalar_prefetch=1,
            grid=(width // dt,),
            in_specs=[pl.BlockSpec(ids_t.shape, lambda i, me: (0, 0))]
            + [
                pl.BlockSpec((len(of_array) * capacity, dt), lambda i, me, block=block: (block, i))
                for _, block, of_array in returned
            ]
            + [pl.BlockSpec((tok_rows, dt), lambda i, me: (0, i)) for _ in held],
            out_specs=pl.BlockSpec((tok_rows, dt), lambda i, me: (0, i)),
            scratch_shapes=[pltpu.VMEM((len(names) * capacity, tok_rows), BF16)],
        ),
        out_shape=jax.ShapeDtypeStruct((tok_rows, width), dtype),
        compiler_params=params(),
        name="combine",
    )(me, ids_t, *[array for array, _, _ in returned], *held)


def per_device(tokens, cotangent, weights, steps, expert_ids):
    groups, parts = lax.axis_size("expert"), lax.axis_size("mp")
    local = weights.shape[0]
    tok_rows, top_k = expert_ids.shape
    capacity = tok_rows // 2
    part = cotangent.shape[2]
    width = tokens.shape[1]
    me, mine = lax.axis_index("expert"), lax.axis_index("mp")
    me_arr = me.astype(jnp.int32)[None]
    mine_arr = mine.astype(jnp.int32)[None]
    expert_swap = lambda x, k: swap(x, "expert", k, groups)
    mp_swap = lambda x, r: swap(x, "mp", r, parts)

    *g_out, own, ids_t, thirds = dispatch(
        me_arr,
        expert_ids.T,
        cotangent.reshape(tok_rows * top_k, part),
        tokens,
        steps,
        groups,
        local,
        capacity,
    )
    near_in = expert_swap(g_out[1], 1)
    g_in = [g_out[0], near_in]
    for k in range(2, groups):
        g_in.append(expert_swap(g_out[k], k))
    of = lambda j, k: g_in[k][j * capacity : (j + 1) * capacity]
    near = [0, 1]
    first = spread(jnp.concatenate([of(j, k) for j in range(local) for k in near] + [thirds], axis=0), parts, False)
    far = {}
    for j in range(local):
        ks = list(range(2, groups))
        if ks:
            rows = jnp.concatenate([of(j, k) for k in ks], axis=0)
            relay = parts == 4 and j == local - 1
            far[j] = [(ks, (spread(rows, parts, relay), rows.shape[0], 0))]
    blocks = [own] + [None] * (groups - 1)
    for k in range(2, groups, 2):
        blocks[k] = expert_swap(own, k)
    for k in range(1, groups, 2):
        blocks[k] = expert_swap(blocks[k - 1], 1)

    pieces = [[] for _ in range(local)]
    at = local * len(near) * capacity
    calls = [[(j, 0, 1) for j in range(local)]]
    calls += [[(0, 1, parts)], [(j, 1, parts) for j in range(1, local)]] if parts > 1 else []
    for call in calls:
        if call:
            outs = quantize(mine_arr, weights, [a[0] for a in first], at, call)
            for m, (j, _, _) in enumerate(call):
                pieces[j].append(outs[3 * m : 3 * m + 3])
    quantized = [[list(a) for a in zip(*of_expert)] for of_expert in pieces]
    rows_t = expert_rows(me_arr, blocks, groups, local, tok_rows, capacity)

    returned, onward, weight_out, partial = [], [], None, []
    scale = QMAX / math.sqrt(width * parts * QMAX)
    for j in range(local):
        values, slopes, step_slopes = quantized[j]
        chunks = [(near, (first, len(near) * capacity, j))] + far.get(j, [])
        ks = [k for of_chunk, _ in chunks for k in of_chunk]
        step = 1 if j == local - 1 else 2
        outs = back_rows([c for _, c in chunks], values, capacity, [step] * (len(ks) // step))
        for k, rows in zip(ks[::step], outs):
            rows = expert_swap(rows, k) if k else in_hbm(rows)
            returned.append((rows, 0, [(j, k)]))
            if step == 2:
                onward.append((rows, j, k + 1))
        weight_out, sums = weight_part(
            mine_arr,
            rows_t[j],
            [c for _, c in chunks],
            slopes,
            step_slopes,
            j,
            weights.shape,
            scale,
            weight_out,
        )
        partial.append(sums)
    for rows, j, k in onward:
        returned.append((expert_swap(rows, 1), 1, [(j, k)]))
    sums = jnp.stack([p.sum(axis=1) for p in partial], axis=1)
    others = [mp_swap(sums[r], r) for r in range(1, parts)]
    step_out = sum(others, sums[0])
    token_out = combine(me_arr, ids_t, returned, groups, local, capacity)
    return (token_out, weight_out, step_out)


def solution(mesh):
    return jax.shard_map(
        per_device,
        mesh=mesh,
        in_specs=(
            P("expert", "mp"),
            P("expert", None, "mp"),
            P("expert", "mp", None),
            P("expert", "mp"),
            P("expert", None),
        ),
        out_specs=(P("expert", "mp"), P("expert", "mp", None), P("expert", "mp")),
        check_vma=False,
    )
```
